256 devices in a mesh: row: 16 (over x, z_hi, core), col: 16 (over z_lo, y).
Axes of the slice: x: 4, y: 4, z: 8 (z_hi: 2, z_lo: 4; z = z_hi * 4 + z_lo), core: 2. Of those that a mesh axis runs over, the one named last changes fastest.
Arguments:
- ancestor_inverse: bfloat16 [24576, 24576], P('row', 'col'), may hold values from -0.0390625 to 0.0390625
- panels: bfloat16 [24576, 3, 512], P(('row', 'col')), may hold values from -1.1953125 to 1.1953125
- diag_inverse: float32 [3, 512, 512], replicated, may hold values from -6 to 6
- tile_mask: int32 [3, 192], replicated, may hold values 0 or 1
Outputs:
- off_diagonal: float32 [24576, 3, 512], P(('row', 'col'))
- diagonal: float32 [3, 512, 512], replicated
The draws below stay inside these ranges and needn't reach their ends.
All inputs are finite; a program needn't handle non-finite values.
Results may differ from the reference program's by a relative error of at most 0.0003.
Values may be sent and summed in bfloat16 or wider, within the bound.
No kernel may reach another device: no remote copies, remote signals or barrier semaphores. Data moves between devices by JAX's collectives and lax.ppermute only.
A program may use at most 192 MiB of HBM per device.

```python
import jax
import jax.numpy as jnp
from jax import lax

ORDER = 24576
WIDTH = 512
PANELS = 3
TILE = 128


def with_ends(entries, key, smallest, largest):
    index_at = [jax.random.randint(jax.random.fold_in(key, axis), (), 0, length) for axis, length in enumerate(entries.shape)]
    widest = entries.shape.index(max(entries.shape))
    beside = index_at[:widest] + [(index_at[widest] + 1) % entries.shape[widest]] + index_at[widest + 1:]
    return entries.at[tuple(index_at)].set(smallest).at[tuple(beside)].set(largest)


def level_of(rng, extent, pieces, low, top_value):
    level, own = 1.0, jax.random.fold_in(rng, 6)
    for dim, shards_of in pieces:
        heights = jnp.exp(jax.random.uniform(jax.random.fold_in(own, dim), (shards_of,), jnp.float32, low / len(pieces), top_value / len(pieces)))
        level = level * jnp.repeat(heights, extent[dim] // shards_of).reshape([-1 if axis == dim else 1 for axis in range(len(extent))])
    return level


def normal_values(own_key, shape, spread, limit, split=(), held_as=jnp.bfloat16):
    factor_of = level_of(own_key, shape, split, -0.22, 0.18) if split else 1.0
    entries = jax.random.normal(own_key, shape, jnp.float32) * spread * factor_of
    return jnp.minimum(jnp.maximum(entries, -limit), limit).astype(held_as)


def setup_inputs(seed: int = 0) -> dict:
    key_of = jax.random.split(jax.random.key(seed), 5)
    return {
        "ancestor_inverse": normal_values(key_of[0], (ORDER, ORDER), ORDER ** -0.5, 0.0390625, ((0, 16), (1, 16))),
        "panels": normal_values(key_of[1], (ORDER, PANELS, WIDTH), 0.2, 1.1953125, ((0, 256),)),
        "diag_inverse": normal_values(key_of[2], (PANELS, WIDTH, WIDTH), 1.0, 6.0, (), jnp.float32),
        "tile_mask": with_ends((jax.random.randint(key_of[3], (PANELS, ORDER // TILE), 0, 2) < 1).astype(jnp.int32), jax.random.fold_in(key_of[3], 1), 0, 1),
    }


def reference(ancestor_inverse, panels, diag_inverse, tile_mask):
    row_mask = jnp.repeat(tile_mask, TILE, axis=1).T.astype(jnp.bfloat16)
    masked = panels * row_mask[:, :, None]
    flattened = masked.reshape(ORDER, PANELS * WIDTH)
    blocks = ancestor_inverse.reshape(16, ORDER // 16, ORDER)

    def product(block):
        return jnp.dot(block, flattened, preferred_element_type=jnp.float32)

    off_diagonal = -lax.map(product, blocks).reshape(ORDER, PANELS, WIDTH)
    schur = jnp.einsum("mpa,mpb->pab", masked.astype(jnp.float32), off_diagonal, precision=lax.Precision.HIGHEST)
    diagonal = diag_inverse - schur
    return off_diagonal, diagonal
```

```python
import jax
import jax.numpy as jnp
from jax import lax
from jax.sharding import PartitionSpec as P

TILE = 128
ALL = ("row", "col")


def body(ancestor_inverse, panels, diag_inverse, tile_mask):
    rows, cols = lax.axis_size("row"), lax.axis_size("col")
    row_index, col_index = lax.axis_index("row"), lax.axis_index("col")
    kept, count, width = panels.shape
    start = (row_index * cols + col_index) * kept
    tile_of = (start + jnp.arange(kept)) // TILE
    own_mask = jnp.take(tile_mask, tile_of, axis=1).astype(jnp.bfloat16)
    masked = jnp.swapaxes(panels, 0, 1) * own_mask[:, :, None]
    flip = [(i * cols + j, j * cols + i) for i in range(rows) for j in range(cols)]
    turned = lax.ppermute(masked, ALL, flip)
    blocks = []
    for p in range(count):
        gathered = lax.all_gather(turned[p], "row", axis=0, tiled=True)
        partial = jnp.dot(ancestor_inverse, gathered, preferred_element_type=jnp.float32)
        summed = lax.psum_scatter(partial, "col", scatter_dimension=0, tiled=True)
        blocks.append(-summed)
    off_diagonal = jnp.stack(blocks)
    schur = jnp.einsum(
        "pma,pmb->pab",
        masked.astype(jnp.float32),
        off_diagonal,
        precision=lax.Precision.HIGHEST,
    )
    lines = schur.reshape(count * width, width)
    share = lax.psum_scatter(lines, "col", scatter_dimension=0, tiled=True)
    share = lax.psum(share, "row")
    total = lax.all_gather(share, "col", axis=0, tiled=True)
    return jnp.swapaxes(off_diagonal, 0, 1), diag_inverse - total.reshape(schur.shape)


def solution(mesh):
    placed = (P("row", "col"), P(ALL, None, None), P(), P())
    return jax.shard_map(
        body, mesh=mesh, in_specs=placed, out_specs=(P(ALL, None, None), P()), check_vma=False
    )
```

```python
import functools

import jax
import jax.numpy as jnp
from jax import lax
from jax.experimental import pallas as pl
from jax.experimental.pallas import tpu as pltpu
from jax.sharding import Mesh
from jax.sharding import PartitionSpec as P

TILE = 128
AXES = ("x", "h", "core", "l", "y")
SIZES = (4, 2, 2, 4, 4)
ROW = ("x", "h", "core")
COL = ("l", "y")
EXTRA = 16
STEPS = 64.0
TOP = 32766.0
LN2 = 0.6931471805599453
VMEM = pl.BlockSpec(memory_space=pltpu.VMEM)
SMEM = pl.BlockSpec(memory_space=pltpu.SMEM)
F32, BF16, I16, I32 = jnp.float32, jnp.bfloat16, jnp.int16, jnp.int32


def coords(device):
    out = []
    for size in SIZES[::-1]:
        out.append(device % size)
        device //= size
    return tuple(out[::-1])


def number(place):
    value = 0
    for size, at in zip(SIZES, place):
        value = value * size + at
    return value


def send(value, move):
    pairs = [(d, number(move(*coords(d)))) for d in range(256)]
    return lax.ppermute(value, AXES, pairs)


def over_x(k):
    return lambda x, h, c, l, y: (x ^ k, h, c, l, y)


def over_y(k):
    return lambda x, h, c, l, y: (x, h, c, l, y ^ k)


def over_l(k):
    return lambda x, h, c, l, y: (x, h, c, l ^ k, y)


def over_h(x, h, c, l, y):
    return (x, 1 - h, c, l, y)


def over_core(x, h, c, l, y):
    return (x, h, 1 - c, l, y)


def spread(x, h, c, l, y):
    return (x ^ l, h, c, l, y)


def turn(i):
    return lambda x, h, c, l, y: (x, (y & 1) ^ i, y >> 1, x ^ l, 2 * h + c)


def params(limit=48):
    return pltpu.CompilerParams(vmem_limit_bytes=limit * 1024 * 1024)


def cost(flops, moved):
    return pl.CostEstimate(flops=flops, bytes_accessed=moved, transcendentals=0)


def diagonal_mask(rows, width):
    row = lax.broadcasted_iota(I32, (rows, width), 0)
    lane = lax.broadcasted_iota(I32, (rows, width), 1)
    return row == lane


def encode(value, out_ref):
    rows, width = value.shape
    largest = jnp.maximum(jnp.max(jnp.abs(value), axis=1, keepdims=True), 1e-30)
    level = jnp.ceil(jnp.log(largest * (1.0 / TOP)) * (STEPS / LN2))
    coded = jnp.round(value * jnp.exp2(level * (-1.0 / STEPS)))
    out_ref[:rows, :] = coded.astype(I32).astype(I16)
    line = jnp.sum(jnp.where(diagonal_mask(rows, width), level, 0.0), axis=0, keepdims=True)
    lines = jnp.broadcast_to(line, (EXTRA, width))
    out_ref[rows : rows + EXTRA, :] = lines.astype(I32).astype(I16)


def decode(in_ref):
    rows, width = in_ref.shape[0] - EXTRA, in_ref.shape[1]
    coded = in_ref[:rows, :].astype(I32).astype(F32)
    line = in_ref[rows : rows + EXTRA, :].astype(I32).astype(F32)[:1]
    level = jnp.sum(
        jnp.where(diagonal_mask(rows, width), jnp.broadcast_to(line, (rows, width)), 0.0),
        axis=1,
        keepdims=True,
    )
    return coded * jnp.exp2(level * (1.0 / STEPS))


def product_kernel(at_ref, a_ref, own_ref, other_ref, keep_ref, q1_ref, q2_ref, q3_ref, m_ref):
    step = pl.program_id(0)
    shard = own_ref.shape[2]

    @pl.when(step == 0)
    def _():
        core, h, t = at_ref[1], at_ref[2], at_ref[3]
        for k in range(4):
            for i in range(2):
                base = (k ^ t) * (4 * shard) + (i ^ h) * shard
                first = pl.multiple_of(base + core * (2 * shard), 32)
                second = pl.multiple_of(base + (1 - core) * (2 * shard), 32)
                m_ref[pl.ds(first, shard), :] = own_ref[k, i]
                m_ref[pl.ds(second, shard), :] = other_ref[k, i]

    block = a_ref[...]
    lines = block.reshape(4 * block.shape[2], block.shape[3])
    value = jnp.dot(lines, m_ref[...], preferred_element_type=F32)

    for at, ref in enumerate((q1_ref, q2_ref, q3_ref)):

        @pl.when(step == at)
        def _(ref=ref):
            encode(value, ref)

    @pl.when(step == 3)
    def _():
        keep_ref[...] = value


def product(at, a4, own, other):
    shard, order = a4.shape[2], a4.shape[3]
    width = own.shape[3]
    rows = 4 * shard
    whole = pl.BlockSpec((4, 2, shard, width), lambda g, s: (0, 0, 0, 0))
    coded = pl.BlockSpec((rows + EXTRA, width), lambda g, s: (0, 0))
    return pl.pallas_call(
        product_kernel,
        grid_spec=pltpu.PrefetchScalarGridSpec(
            num_scalar_prefetch=1,
            grid=(4,),
            in_specs=[
                pl.BlockSpec(
                    (4, 1, shard, order), lambda g, s: (0, s[0] ^ ((g + 1) & 3), 0, 0)
                ),
                whole,
                whole,
            ],
            out_specs=[pl.BlockSpec((rows, width), lambda g, s: (0, 0))] + [coded] * 3,
            scratch_shapes=[pltpu.VMEM((order, width), BF16)],
        ),
        out_shape=[jax.ShapeDtypeStruct((rows, width), F32)]
        + [jax.ShapeDtypeStruct((rows + EXTRA, width), I16)] * 3,
        compiler_params=params(),
        cost_estimate=cost(8 * rows * order * width, 2 * order * order),
        name="product",
    )(at, a4, own, other)


def middle_kernel(at_ref, keep_ref, r1_ref, r2_ref, r3_ref, own_ref, q1_ref, q2_ref, q3_ref, sum_ref):
    shard = own_ref.shape[0]
    sum_ref[...] = ((keep_ref[...] + decode(r1_ref)) + decode(r2_ref)) + decode(r3_ref)
    l = at_ref[4]

    def part(k):
        return sum_ref[pl.ds(pl.multiple_of((l ^ k) * shard, 32), shard), :]

    own_ref[...] = part(0)
    for k, ref in ((1, q1_ref), (2, q2_ref), (3, q3_ref)):
        encode(part(k), ref)


def middle(at, keep, parts):
    rows, width = keep.shape
    shard = rows // 4
    return pl.pallas_call(
        middle_kernel,
        in_specs=[SMEM] + [VMEM] * 4,
        out_specs=[VMEM] * 4,
        out_shape=[jax.ShapeDtypeStruct((shard, width), F32)]
        + [jax.ShapeDtypeStruct((shard + EXTRA, width), I16)] * 3,
        scratch_shapes=[pltpu.VMEM((rows, width), F32)],
        compiler_params=params(),
        cost_estimate=cost(8 * rows * width, 16 * rows * width),
        name="middle",
    )(at, keep, *parts)


def last_kernel(at_ref, own_ref, r1_ref, r2_ref, r3_ref, masked_ref, out_ref, mine_ref, theirs_ref):
    total = -(((own_ref[...] + decode(r1_ref)) + decode(r2_ref)) + decode(r3_ref))
    out_ref[...] = total
    high = total.astype(BF16)
    rest = total - high.astype(F32)
    mid = rest.astype(BF16)
    low = (rest - mid.astype(F32)).astype(BF16)
    core = at_ref[1]
    half = mine_ref.shape[0]

    def schur(which):
        left = masked_ref[:, pl.ds(pl.multiple_of(which * half, 128), half)]
        dims = (((0,), (0,)), ((), ()))
        parts = [lax.dot_general(left, r, dims, preferred_element_type=F32) for r in (low, mid, high)]
        return (parts[0] + parts[1]) + parts[2]

    mine_ref[...] = schur(core)
    theirs_ref[...] = schur(1 - core)


def last(at, own, parts, masked):
    rows, width = own.shape
    return pl.pallas_call(
        last_kernel,
        in_specs=[SMEM] + [VMEM] * 5,
        out_specs=[VMEM] * 3,
        out_shape=[jax.ShapeDtypeStruct((rows, width), F32)]
        + [jax.ShapeDtypeStruct((width // 2, width), F32)] * 2,
        compiler_params=params(),
        cost_estimate=cost(6 * rows * width * width, 4 * width * width),
        name="last",
    )(at, own, *parts, masked)


def fold_kernel(which, count, at_ref, *refs):
    ins, outs = refs[:count], refs[count:]
    rows = outs[0].shape[0]
    for k, out in enumerate(outs):
        place = pl.ds(pl.multiple_of((at_ref[which] ^ k) * rows, 8), rows)
        total = ins[0][place, :]
        for ref in ins[1:]:
            total = total + ref[place, :]
        out[...] = total


def fold(at, which, ins):
    rows, width = ins[0].shape
    return pl.pallas_call(
        functools.partial(fold_kernel, which, len(ins)),
        in_specs=[SMEM] + [VMEM] * len(ins),
        out_specs=[VMEM] * 4,
        out_shape=[jax.ShapeDtypeStruct((rows // 4, width), F32)] * 4,
        compiler_params=params(),
        cost_estimate=cost(rows * width, 8 * rows * width),
        name="fold",
    )(at, *ins)


def join_kernel(which, at_ref, *refs):
    ins, out = refs[:-1], refs[-1]
    rows = ins[0].shape[0]
    for k, ref in enumerate(ins):
        out[pl.ds(pl.multiple_of((at_ref[which] ^ k) * rows, 8), rows), :] = ref[...]


def join(at, which, ins):
    rows, width = ins[0].shape
    return pl.pallas_call(
        functools.partial(join_kernel, which),
        in_specs=[SMEM] + [VMEM] * len(ins),
        out_specs=VMEM,
        out_shape=jax.ShapeDtypeStruct((len(ins) * rows, width), F32),
        compiler_params=params(),
        cost_estimate=cost(rows * width, 8 * rows * width),
        name="join",
    )(at, *ins)


def finish_kernel(at_ref, mine_ref, theirs_ref, diag_ref, out_ref):
    half = diag_ref.shape[1] // 2
    core = at_ref[1]
    for p in range(diag_ref.shape[0]):
        for which, ref in ((core, mine_ref), (1 - core, theirs_ref)):
            place = pl.ds(pl.multiple_of(which * half, 8), half)
            out_ref[p, place, :] = diag_ref[p, place, :] - ref[p * half : (p + 1) * half, :]


def finish(at, mine, theirs, diag):
    return pl.pallas_call(
        finish_kernel,
        in_specs=[SMEM] + [VMEM] * 3,
        out_specs=VMEM,
        out_shape=jax.ShapeDtypeStruct(diag.shape, F32),
        compiler_params=params(),
        cost_estimate=cost(diag.size, 12 * diag.size),
        name="finish",
    )(at, mine, theirs, diag)


def body(ancestor_inverse, panels, diag_inverse, tile_mask):
    x, h, core, l, y = (lax.axis_index(axis) for axis in AXES)
    at = jnp.stack([y, core, h, x ^ l, l, x]).astype(I32)
    kept, count, width = panels.shape
    order = ancestor_inverse.shape[1]
    tiles = tile_mask.shape[1]
    start = (((x * 2 + h) * 2 + core) * 16 + l * 4 + y) * kept
    tile = start // TILE
    first = lax.dynamic_slice_in_dim(tile_mask, tile, 1, 1)
    second = lax.dynamic_slice_in_dim(tile_mask, jnp.minimum(tile + 1, tiles - 1), 1, 1)
    in_first = start + jnp.arange(kept) < (tile + 1) * TILE
    own_mask = jnp.where(in_first[None, :], first, second).astype(BF16)
    masked = jnp.swapaxes(panels, 0, 1) * own_mask[:, :, None]

    moved = send(masked, spread)
    turned = [send(moved, turn(i)) for i in range(2)]
    a4 = ancestor_inverse.reshape(4, 4, kept, order)
    blocks, mines, theirs = [], [], []
    for p in range(count):
        message = jnp.stack([turned[0][p], turned[1][p]])
        own = jnp.stack([message] + [send(message, over_x(k)) for k in (1, 2, 3)])
        other = send(own, over_core)
        keep, *coded = product(at, a4, own, other)
        parts = [send(coded[k - 1], over_y(k)) for k in (1, 2, 3)]
        keep, *coded = middle(at, keep, parts)
        parts = [send(coded[k - 1], over_l(k)) for k in (1, 2, 3)]
        block, mine, their = last(at, keep, parts, masked[p])
        blocks.append(block)
        mines.append(mine)
        theirs.append(their)

    finals = []
    for group in ((0, 1), (2,)):
        mine = jnp.concatenate([mines[p] for p in group])
        their = jnp.concatenate([theirs[p] for p in group])
        pieces = fold(at, 5, [mine, send(their, over_core)])
        pieces = fold(at, 0, [pieces[0]] + [send(pieces[k], over_x(k)) for k in (1, 2, 3)])
        total = ((pieces[0] + send(pieces[1], over_y(1))) + send(pieces[2], over_y(2))) + send(
            pieces[3], over_y(3)
        )
        total = total + send(total, over_h)
        total = total + send(total, over_l(1))
        total = total + send(total, over_l(2))
        total = join(at, 0, [total] + [send(total, over_y(k)) for k in (1, 2, 3)])
        total = join(at, 5, [total] + [send(total, over_x(k)) for k in (1, 2, 3)])
        diag = diag_inverse[group[0] : group[-1] + 1]
        finals.append(finish(at, total, send(total, over_core), diag))
    off_diagonal = jnp.swapaxes(jnp.stack(blocks), 0, 1)
    return off_diagonal, jnp.concatenate(finals)


def solution(mesh):
    finer = Mesh(mesh.devices.reshape(SIZES), AXES)
    placed = (P(ROW, COL), P(AXES, None, None), P(), P())
    return jax.shard_map(
        body, mesh=finer, in_specs=placed, out_specs=(P(AXES, None, None), P()), check_vma=False
    )
```

```python
import functools

import jax
import jax.numpy as jnp
from jax import lax
from jax.experimental import pallas as pl
from jax.experimental.pallas import tpu as pltpu
from jax.sharding import Mesh
from jax.sharding import PartitionSpec as P

TILE = 128
AXES = ("x", "h", "core", "l", "y")
SIZES = (4, 2, 2, 4, 4)
ROW = ("x", "h", "core")
COL = ("l", "y")
EXTRA = 16
STEPS = 64.0
TOP = 32766.0
LN2 = 0.6931471805599453
VMEM = pl.BlockSpec(memory_space=pltpu.VMEM)
SMEM = pl.BlockSpec(memory_space=pltpu.SMEM)
F32, BF16, I16, I32 = jnp.float32, jnp.bfloat16, jnp.int16, jnp.int32


def coords(device):
    out = []
    for size in SIZES[::-1]:
        out.append(device % size)
        device //= size
    return tuple(out[::-1])


def number(place):
    value = 0
    for size, at in zip(SIZES, place):
        value = value * size + at
    return value


def send(value, move):
    pairs = [(d, number(move(*coords(d)))) for d in range(256)]
    return lax.ppermute(value, AXES, pairs)


def over_x(k):
    return lambda x, h, c, l, y: (x ^ k, h, c, l, y)


def over_y(k):
    return lambda x, h, c, l, y: (x, h, c, l, y ^ k)


def over_l(k):
    return lambda x, h, c, l, y: (x, h, c, l ^ k, y)


def over_h(x, h, c, l, y):
    return (x, 1 - h, c, l, y)


def over_core(x, h, c, l, y):
    return (x, h, 1 - c, l, y)


def spread(x, h, c, l, y):
    return (x ^ l, h, c, l, y)


def turn(i):
    return lambda x, h, c, l, y: (x, (y & 1) ^ i, y >> 1, x ^ l, 2 * h + c)


def params(limit=48):
    return pltpu.CompilerParams(vmem_limit_bytes=limit * 1024 * 1024)


def cost(flops, moved):
    return pl.CostEstimate(flops=flops // 1000, bytes_accessed=moved // 1000, transcendentals=0)


def diagonal_mask(rows, width):
    row = lax.broadcasted_iota(I32, (rows, width), 0)
    lane = lax.broadcasted_iota(I32, (rows, width), 1)
    return row == lane


def encode(value, out_ref, start=0):
    rows, width = value.shape
    largest = jnp.maximum(jnp.max(jnp.abs(value), axis=1, keepdims=True), 1e-30)
    level = jnp.ceil(jnp.log(largest * (1.0 / TOP)) * (STEPS / LN2))
    coded = jnp.round(value * jnp.exp2(level * (-1.0 / STEPS)))
    out_ref[start : start + rows, :] = coded.astype(I32).astype(I16)
    line = jnp.sum(jnp.where(diagonal_mask(rows, width), level, 0.0), axis=0, keepdims=True)
    lines = jnp.broadcast_to(line, (EXTRA, width))
    out_ref[start + rows : start + rows + EXTRA, :] = lines.astype(I32).astype(I16)


def decode(in_ref, start=0, rows=None):
    rows, width = rows or in_ref.shape[0] - EXTRA, in_ref.shape[1]
    coded = in_ref[start : start + rows, :].astype(I32).astype(F32)
    line = in_ref[start + rows : start + rows + EXTRA, :].astype(I32).astype(F32)[:1]
    level = jnp.sum(
        jnp.where(diagonal_mask(rows, width), jnp.broadcast_to(line, (rows, width)), 0.0),
        axis=1,
        keepdims=True,
    )
    return coded * jnp.exp2(level * (1.0 / STEPS))


def product_kernel(at_ref, a_ref, own_ref, other_ref, keep_ref, q1_ref, q2_ref, q3_ref, m_ref):
    step = pl.program_id(0)
    shard = own_ref.shape[2]

    @pl.when(step == 0)
    def _():
        core, h, t = at_ref[1], at_ref[2], at_ref[3]
        for k in range(4):
            for i in range(2):
                base = (k ^ t) * (4 * shard) + (i ^ h) * shard
                first = pl.multiple_of(base + core * (2 * shard), 32)
                second = pl.multiple_of(base + (1 - core) * (2 * shard), 32)
                m_ref[pl.ds(first, shard), :] = own_ref[k, i]
                m_ref[pl.ds(second, shard), :] = other_ref[k, i]

    block = a_ref[...]
    lines = block.reshape(4 * block.shape[2], block.shape[3])
    value = jnp.dot(lines, m_ref[...], preferred_element_type=F32)

    for at, ref in enumerate((q1_ref, q2_ref, q3_ref)):

        @pl.when(step == at)
        def _(ref=ref):
            encode(value, ref)

    @pl.when(step == 3)
    def _():
        keep_ref[...] = value


def product(at, a4, own, other):
    shard, order = a4.shape[2], a4.shape[3]
    width = own.shape[3]
    rows = 4 * shard
    whole = pl.BlockSpec((4, 2, shard, width), lambda g, s: (0, 0, 0, 0))
    coded = pl.BlockSpec((rows + EXTRA, width), lambda g, s: (0, 0))
    return pl.pallas_call(
        product_kernel,
        grid_spec=pltpu.PrefetchScalarGridSpec(
            num_scalar_prefetch=1,
            grid=(4,),
            in_specs=[
                pl.BlockSpec(
                    (4, 1, shard, order), lambda g, s: (0, s[0] ^ ((g + 1) & 3), 0, 0)
                ),
                whole,
                whole,
            ],
            out_specs=[pl.BlockSpec((rows, width), lambda g, s: (0, 0))] + [coded] * 3,
            scratch_shapes=[pltpu.VMEM((order, width), BF16)],
        ),
        out_shape=[jax.ShapeDtypeStruct((rows, width), F32)]
        + [jax.ShapeDtypeStruct((rows + EXTRA, width), I16)] * 3,
        compiler_params=params(),
        cost_estimate=cost(8 * rows * order * width, 2 * order * order),
        name="product",
    )(at, a4, own, other)


def middle_kernel(panels, *refs):
    at_ref, refs = refs[0], refs[1:]
    keeps, refs = refs[:panels], refs[panels:]
    parts, refs = refs[: 3 * panels], refs[3 * panels :]
    own_ref, *coded = refs[:4]
    sum_ref = refs[4]
    shard = own_ref.shape[0] // panels
    l = at_ref[4]

    def part(k):
        return sum_ref[pl.ds(pl.multiple_of((l ^ k) * shard, 32), shard), :]

    for p in range(panels):
        value = keeps[p][...]
        for ref in parts[3 * p : 3 * p + 3]:
            value = value + decode(ref)
        sum_ref[...] = value
        own_ref[p * shard : (p + 1) * shard, :] = part(0)
        for k in (1, 2, 3):
            encode(part(k), coded[k - 1], p * (shard + EXTRA))


def middle(at, keeps, parts):
    rows, width = keeps[0].shape
    panels, shard = len(keeps), rows // 4
    return pl.pallas_call(
        functools.partial(middle_kernel, panels),
        in_specs=[SMEM] + [VMEM] * (4 * panels),
        out_specs=[VMEM] * 4,
        out_shape=[jax.ShapeDtypeStruct((panels * shard, width), F32)]
        + [jax.ShapeDtypeStruct((panels * (shard + EXTRA), width), I16)] * 3,
        scratch_shapes=[pltpu.VMEM((rows, width), F32)],
        compiler_params=params(),
        cost_estimate=cost(8 * rows * width, 16 * rows * width),
        name="middle",
    )(at, *keeps, *sum(parts, []))


def last_kernel(panels, at_ref, own_ref, r1_ref, r2_ref, r3_ref, masked_ref, out_ref, mine_ref, theirs_ref):
    shard = out_ref.shape[1]
    half = mine_ref.shape[0] // panels
    core = at_ref[1]
    for p in range(panels):
        total = own_ref[p * shard : (p + 1) * shard, :]
        for ref in (r1_ref, r2_ref, r3_ref):
            total = total + decode(ref, p * (shard + EXTRA), shard)
        total = -total
        out_ref[p] = total
        high = total.astype(BF16)
        rest = total - high.astype(F32)
        mid = rest.astype(BF16)
        low = (rest - mid.astype(F32)).astype(BF16)
        for which, out in ((core, mine_ref), (1 - core, theirs_ref)):
            left = masked_ref[p, :, pl.ds(pl.multiple_of(which * half, 128), half)]
            dims = (((0,), (0,)), ((), ()))
            terms = [
                lax.dot_general(left, r, dims, preferred_element_type=F32) for r in (low, mid, high)
            ]
            out[p * half : (p + 1) * half, :] = (terms[0] + terms[1]) + terms[2]


def last(at, own, parts, masked):
    panels, shard, width = masked.shape
    return pl.pallas_call(
        functools.partial(last_kernel, panels),
        in_specs=[SMEM] + [VMEM] * 5,
        out_specs=[VMEM] * 3,
        out_shape=[jax.ShapeDtypeStruct((panels, shard, width), F32)]
        + [jax.ShapeDtypeStruct((panels * (width // 2), width), F32)] * 2,
        compiler_params=params(),
        cost_estimate=cost(6 * shard * width * width, 16 * shard * width),
        name="last",
    )(at, own, *parts, masked)


def fold_kernel(*refs):
    out, count = refs[-1], len(refs) // 2
    start = 0
    for p in range(count):
        rows = refs[p].shape[0]
        out[start : start + rows, :] = refs[p][...] + refs[count + p][...]
        start += rows


def fold(mines, theirs):
    width = mines[0].shape[1]
    total = sum(mine.shape[0] for mine in mines)
    return pl.pallas_call(
        fold_kernel,
        in_specs=[VMEM] * (2 * len(mines)),
        out_specs=VMEM,
        out_shape=jax.ShapeDtypeStruct((total, width), F32),
        compiler_params=params(),
        cost_estimate=cost(total * width, 12 * total * width),
        name="fold",
    )(*mines, *theirs)


def finish_kernel(at_ref, mine_ref, theirs_ref, diag_ref, out_ref):
    half = diag_ref.shape[1] // 2
    core = at_ref[1]
    for p in range(diag_ref.shape[0]):
        for which, ref in ((core, mine_ref), (1 - core, theirs_ref)):
            place = pl.ds(pl.multiple_of(which * half, 8), half)
            out_ref[p, place, :] = diag_ref[p, place, :] - ref[p * half : (p + 1) * half, :]


def finish(at, mine, theirs, diag):
    return pl.pallas_call(
        finish_kernel,
        in_specs=[SMEM] + [VMEM] * 3,
        out_specs=VMEM,
        out_shape=jax.ShapeDtypeStruct(diag.shape, F32),
        compiler_params=params(),
        cost_estimate=cost(diag.size, 12 * diag.size),
        name="finish",
    )(at, mine, theirs, diag)


def after(values, *earlier):
    return lax.optimization_barrier((values, earlier))[0]


def body(ancestor_inverse, panels, diag_inverse, tile_mask):
    x, h, core, l, y = (lax.axis_index(axis) for axis in AXES)
    at = jnp.stack([y, core, h, x ^ l, l, x]).astype(I32)
    kept, count, width = panels.shape
    order = ancestor_inverse.shape[1]
    tiles = tile_mask.shape[1]
    start = (((x * 2 + h) * 2 + core) * 16 + l * 4 + y) * kept
    tile = start // TILE
    first = lax.dynamic_slice_in_dim(tile_mask, tile, 1, 1)
    second = lax.dynamic_slice_in_dim(tile_mask, jnp.minimum(tile + 1, tiles - 1), 1, 1)
    in_first = start + jnp.arange(kept) < (tile + 1) * TILE
    own_mask = jnp.where(in_first[None, :], first, second).astype(BF16)
    masked = jnp.swapaxes(panels, 0, 1) * own_mask[:, :, None]

    moved = send(masked, spread)
    turned = [send(moved, turn(i)) for i in range(2)]
    a4 = ancestor_inverse.reshape(4, 4, kept, order)
    def gather(messages):
        found = [send(messages, over_x(k)) for k in (1, 2, 3)]
        return jnp.stack([messages] + found, axis=1)

    messages = jnp.stack([turned[0], turned[1]], axis=1)
    own_a = gather(messages[:1])
    other_a = send(own_a, over_core)
    rest = after(messages[1:], own_a)
    keep, *coded = product(at, a4, own_a[0], other_a[0])
    keeps = [keep]
    parts = [[send(coded[k - 1], over_y(k)) for k in (1, 2, 3)]]
    found = after([send(rest, over_x(k)) for k in (1, 2, 3)], keep)
    own_b = jnp.stack([rest] + found, axis=1)
    other_b = send(own_b, over_core)
    for p in (1, 2):
        own = own_b[p - 1]
        keep, *coded = product(at, a4, own, other_b[p - 1])
        keeps.append(keep)
        parts.append([send(coded[k - 1], over_y(k)) for k in (1, 2, 3)])
    parts[:2] = after(parts[:2], keeps[2], parts[2][0])
    own_01, *coded = middle(at, keeps[:2], parts[:2])
    found = [send(coded[k - 1], over_l(k)) for k in (1, 2, 3)]
    block_01, mine_01, their_01 = last(at, own_01, found, masked[:2])
    swapped_01 = send(their_01, over_core)
    parts[2] = after(parts[2], their_01)
    own_2, *coded = middle(at, keeps[2:], parts[2:])
    found = [send(coded[k - 1], over_l(k)) for k in (1, 2, 3)]
    block_2, mine_2, their_2 = last(at, own_2, found, masked[2:])
    halves = fold([mine_01, mine_2], [swapped_01, send(their_2, over_core)])
    pieces = halves.reshape(16, -1, width)
    total = jnp.sum(lax.all_to_all(pieces, ("x", "y"), 0, 0), axis=0)
    total = total + send(total, over_h)
    total = total + send(total, over_l(1))
    total = total + send(total, over_l(2))
    pieces = jnp.broadcast_to(total[None], (16, *total.shape))
    mine = lax.all_to_all(pieces, ("x", "y"), 0, 0).reshape(halves.shape)
    diagonal = finish(at, mine, send(mine, over_core), diag_inverse)
    off_diagonal = jnp.swapaxes(jnp.concatenate([block_01, block_2]), 0, 1)
    return off_diagonal, diagonal


def solution(mesh):
    finer = Mesh(mesh.devices.reshape(SIZES), AXES)
    placed = (P(ROW, COL), P(AXES, None, None), P(), P())
    return jax.shard_map(
        body, mesh=finer, in_specs=placed, out_specs=(P(AXES, None, None), P()), check_vma=False
    )
```

```python
import functools

import jax
import jax.numpy as jnp
from jax import lax
from jax.experimental import pallas as pl
from jax.experimental.pallas import tpu as pltpu
from jax.sharding import Mesh
from jax.sharding import PartitionSpec as P

TILE = 128
AXES = ("x", "h", "core", "l", "y")
SIZES = (4, 2, 2, 4, 4)
ROW = ("x", "h", "core")
COL = ("l", "y")
EXTRA = 16
STEPS = 64.0
TOP = 32766.0
LN2 = 0.6931471805599453
VMEM = pl.BlockSpec(memory_space=pltpu.VMEM)
SMEM = pl.BlockSpec(memory_space=pltpu.SMEM)
F32, BF16, I16, I32 = jnp.float32, jnp.bfloat16, jnp.int16, jnp.int32


def coords(device):
    out = []
    for size in SIZES[::-1]:
        out.append(device % size)
        device //= size
    return tuple(out[::-1])


def number(place):
    value = 0
    for size, at in zip(SIZES, place):
        value = value * size + at
    return value


def send(value, move):
    pairs = [(d, number(move(*coords(d)))) for d in range(256)]
    return lax.ppermute(value, AXES, pairs)


def over_x(k):
    return lambda x, h, c, l, y: (x ^ k, h, c, l, y)


def over_y(k):
    return lambda x, h, c, l, y: (x, h, c, l, y ^ k)


def over_l(k):
    return lambda x, h, c, l, y: (x, h, c, l ^ k, y)


def over_h(x, h, c, l, y):
    return (x, 1 - h, c, l, y)


def over_core(x, h, c, l, y):
    return (x, h, 1 - c, l, y)


def spread(x, h, c, l, y):
    return (x ^ l, h, c, l, y)


def turn(i):
    return lambda x, h, c, l, y: (x, (y & 1) ^ i, y >> 1, x ^ l, 2 * h + c)


def params(limit=20):
    return pltpu.CompilerParams(vmem_limit_bytes=limit * 1024 * 1024)


def cost(flops, moved):
    return pl.CostEstimate(flops=flops // 1000, bytes_accessed=moved // 1000, transcendentals=0)


def diagonal_mask(rows, width):
    row = lax.broadcasted_iota(I32, (rows, width), 0)
    lane = lax.broadcasted_iota(I32, (rows, width), 1)
    return row == lane


def encode(value, out_ref, start=0):
    rows, width = value.shape
    largest = jnp.maximum(jnp.max(jnp.abs(value), axis=1, keepdims=True), 1e-30)
    level = jnp.ceil(jnp.log(largest * (1.0 / TOP)) * (STEPS / LN2))
    coded = jnp.round(value * jnp.exp2(level * (-1.0 / STEPS)))
    out_ref[start : start + rows, :] = coded.astype(I32).astype(I16)
    line = jnp.sum(jnp.where(diagonal_mask(rows, width), level, 0.0), axis=0, keepdims=True)
    lines = jnp.broadcast_to(line, (EXTRA, width))
    out_ref[start + rows : start + rows + EXTRA, :] = lines.astype(I32).astype(I16)


def decode(in_ref, start=0, rows=None):
    rows, width = rows or in_ref.shape[0] - EXTRA, in_ref.shape[1]
    coded = in_ref[start : start + rows, :].astype(I32).astype(F32)
    line = in_ref[start + rows : start + rows + EXTRA, :].astype(I32).astype(F32)[:1]
    level = jnp.sum(
        jnp.where(diagonal_mask(rows, width), jnp.broadcast_to(line, (rows, width)), 0.0),
        axis=1,
        keepdims=True,
    )
    return coded * jnp.exp2(level * (1.0 / STEPS))


def product_kernel(panels, at_ref, a_ref, own_ref, other_ref, *refs):
    outs, m_ref = refs[: 4 * panels], refs[4 * panels]
    step = pl.program_id(0)
    shard = own_ref.shape[3]

    @pl.when(step == 0)
    def _():
        core, h, t = at_ref[1], at_ref[2], at_ref[3]
        for p in range(panels):
            for k in range(4):
                for i in range(2):
                    base = (k ^ t) * (4 * shard) + (i ^ h) * shard
                    first = pl.multiple_of(base + core * (2 * shard), 32)
                    second = pl.multiple_of(base + (1 - core) * (2 * shard), 32)
                    m_ref[p, pl.ds(first, shard), :] = own_ref[k, i, p]
                    m_ref[p, pl.ds(second, shard), :] = other_ref[k, i, p]

    block = a_ref[...]
    lines = block.reshape(4 * block.shape[2], block.shape[3])
    for p in range(panels):
        value = jnp.dot(lines, m_ref[p], preferred_element_type=F32)
        for at in range(3):

            @pl.when(step == at)
            def _(ref=outs[4 * p + 1 + at], value=value):
                encode(value, ref)

        @pl.when(step == 3)
        def _(ref=outs[4 * p], value=value):
            ref[...] = value


def product(at, a4, own, other, first, panels):
    shard, order = a4.shape[2], a4.shape[3]
    width = own.shape[4]
    rows = 4 * shard
    whole = pl.BlockSpec((4, 2, panels, shard, width), lambda g, s: (0, 0, first // panels, 0, 0))
    kept = pl.BlockSpec((rows, width), lambda g, s: (0, 0))
    coded = pl.BlockSpec((rows + EXTRA, width), lambda g, s: (0, 0))
    one = [jax.ShapeDtypeStruct((rows, width), F32)]
    one += [jax.ShapeDtypeStruct((rows + EXTRA, width), I16)] * 3
    outs = pl.pallas_call(
        functools.partial(product_kernel, panels),
        grid_spec=pltpu.PrefetchScalarGridSpec(
            num_scalar_prefetch=1,
            grid=(4,),
            in_specs=[
                pl.BlockSpec(
                    (4, 1, shard, order), lambda g, s: (0, s[0] ^ ((g + 1) & 3), 0, 0)
                ),
                whole,
                whole,
            ],
            out_specs=([kept] + [coded] * 3) * panels,
            scratch_shapes=[pltpu.VMEM((panels, order, width), BF16)],
        ),
        out_shape=one * panels,
        compiler_params=params(),
        cost_estimate=cost(8 * panels * rows * order * width, 2 * order * order),
        name="product",
    )(at, a4, own, other)
    return [outs[4 * p : 4 * p + 4] for p in range(panels)]


def middle_kernel(panels, base, *refs):
    at_ref, refs = refs[0], refs[1:]
    keeps, refs = refs[:panels], refs[panels:]
    parts, refs = refs[: 3 * panels], refs[3 * panels :]
    masked, refs = refs[:4], refs[4:]
    own_ref, *coded = refs[:4]
    mine_ref, theirs_ref, sum_ref, m_ref = refs[4:]
    shard = own_ref.shape[0] // panels
    half = mine_ref.shape[0] // panels
    core, l = at_ref[1], at_ref[4]

    def place(k):
        return pl.ds(pl.multiple_of((l ^ k) * shard, 32), shard)

    for p in range(panels):
        value = keeps[p][...]
        for ref in parts[3 * p : 3 * p + 3]:
            value = value + decode(ref)
        sum_ref[...] = value
        own_ref[p * shard : (p + 1) * shard, :] = sum_ref[place(0), :]
        for k in (1, 2, 3):
            encode(sum_ref[place(k), :], coded[k - 1], p * (shard + EXTRA))
        for k, ref in enumerate(masked):
            m_ref[place(k), :] = ref[base + p]
        high = value.astype(BF16)
        rest = value - high.astype(F32)
        mid = rest.astype(BF16)
        low = (rest - mid.astype(F32)).astype(BF16)
        for which, out in ((core, mine_ref), (1 - core, theirs_ref)):
            left = m_ref[:, pl.ds(pl.multiple_of(which * half, 128), half)]
            dims = (((0,), (0,)), ((), ()))
            terms = [
                lax.dot_general(left, r, dims, preferred_element_type=F32) for r in (low, mid, high)
            ]
            out[p * half : (p + 1) * half, :] = (terms[0] + terms[1]) + terms[2]


def middle(at, keeps, parts, masked, base):
    rows, width = keeps[0].shape
    panels, shard = len(keeps), rows // 4
    return pl.pallas_call(
        functools.partial(middle_kernel, panels, base),
        in_specs=[SMEM] + [VMEM] * (4 * panels + 4),
        out_specs=[VMEM] * 6,
        out_shape=[jax.ShapeDtypeStruct((panels * shard, width), F32)]
        + [jax.ShapeDtypeStruct((panels * (shard + EXTRA), width), I16)] * 3
        + [jax.ShapeDtypeStruct((panels * (width // 2), width), F32)] * 2,
        scratch_shapes=[pltpu.VMEM((rows, width), F32), pltpu.VMEM((rows, width), BF16)],
        compiler_params=params(),
        cost_estimate=cost(6 * rows * width * width, 16 * rows * width),
        name="middle",
    )(at, *keeps, *sum(parts, []), *masked)


def last_kernel(panels, own_ref, r1_ref, r2_ref, r3_ref, out_ref):
    shard = out_ref.shape[1]
    for p in range(panels):
        total = own_ref[p * shard : (p + 1) * shard, :]
        for ref in (r1_ref, r2_ref, r3_ref):
            total = total + decode(ref, p * (shard + EXTRA), shard)
        out_ref[p] = -total


def last(panels, own, parts):
    rows, width = own.shape
    return pl.pallas_call(
        functools.partial(last_kernel, panels),
        in_specs=[VMEM] * 4,
        out_specs=VMEM,
        out_shape=jax.ShapeDtypeStruct((panels, rows // panels, width), F32),
        compiler_params=params(),
        cost_estimate=cost(8 * rows * width, 16 * rows * width),
        name="last",
    )(own, *parts)


def fold_kernel(*refs):
    out, count = refs[-1], len(refs) // 2
    start = 0
    for p in range(count):
        rows = refs[p].shape[0]
        out[start : start + rows, :] = refs[p][...] + refs[count + p][...]
        start += rows


def fold(mines, theirs):
    width = mines[0].shape[1]
    total = sum(mine.shape[0] for mine in mines)
    return pl.pallas_call(
        fold_kernel,
        in_specs=[VMEM] * (2 * len(mines)),
        out_specs=VMEM,
        out_shape=jax.ShapeDtypeStruct((total, width), F32),
        compiler_params=params(),
        cost_estimate=cost(total * width, 12 * total * width),
        name="fold",
    )(*mines, *theirs)


def finish_kernel(at_ref, mine_ref, theirs_ref, diag_ref, out_ref):
    half = diag_ref.shape[1] // 2
    core = at_ref[1]
    for p in range(diag_ref.shape[0]):
        for which, ref in ((core, mine_ref), (1 - core, theirs_ref)):
            place = pl.ds(pl.multiple_of(which * half, 8), half)
            out_ref[p, place, :] = diag_ref[p, place, :] + ref[p * half : (p + 1) * half, :]


def finish(at, mine, theirs, diag):
    return pl.pallas_call(
        finish_kernel,
        in_specs=[SMEM] + [VMEM] * 3,
        out_specs=VMEM,
        out_shape=jax.ShapeDtypeStruct(diag.shape, F32),
        compiler_params=params(),
        cost_estimate=cost(diag.size, 12 * diag.size),
        name="finish",
    )(at, mine, theirs, diag)


def after(values, *earlier):
    return lax.optimization_barrier((values, earlier))[0]


def body(ancestor_inverse, panels, diag_inverse, tile_mask):
    x, h, core, l, y = (lax.axis_index(axis) for axis in AXES)
    at = jnp.stack([y, core, h, x ^ l, l, x]).astype(I32)
    kept, count, width = panels.shape
    order = ancestor_inverse.shape[1]
    tiles = tile_mask.shape[1]
    start = (((x * 2 + h) * 2 + core) * 16 + l * 4 + y) * kept
    tile = start // TILE
    first = lax.dynamic_slice_in_dim(tile_mask, tile, 1, 1)
    second = lax.dynamic_slice_in_dim(tile_mask, jnp.minimum(tile + 1, tiles - 1), 1, 1)
    in_first = start + jnp.arange(kept) < (tile + 1) * TILE
    own_mask = jnp.where(in_first[None, :], first, second).astype(BF16)
    masked = jnp.swapaxes(panels, 0, 1) * own_mask[:, :, None]

    moved = send(masked, spread)
    turned = [send(moved, turn(i)) for i in range(2)]
    late = after(masked, turned)
    beside = [masked] + [send(late, over_l(k)) for k in (1, 2, 3)]
    a4 = ancestor_inverse.reshape(4, 4, kept, order)
    message = jnp.stack(turned)
    found = [send(message, over_x(k)) for k in (1, 2, 3)]
    own = after(jnp.stack([message] + found), beside)
    other = send(own, over_core)
    keeps, parts = [], []
    for group in ((2,), (0, 1)):
        for keep, *coded in product(at, a4, own, other, group[0], len(group)):
            keeps.append(keep)
            parts.append(coded)
        if len(group) == 1:
            parts[0] = [send(parts[0][k - 1], over_y(k)) for k in (1, 2, 3)]
    pairs = [jnp.stack([parts[1][k], parts[2][k]]) for k in range(3)]
    pairs = after(pairs, parts[0])
    pairs = [send(pairs[k - 1], over_y(k)) for k in (1, 2, 3)]
    own_2, *coded = middle(at, keeps[:1], parts[:1], beside, 2)
    coded_2, (mine_2, their_2) = coded[:3], coded[3:]
    swapped_2 = send(their_2, over_core)
    pairs = after(pairs, mine_2)
    parts = [[pair[p] for pair in pairs] for p in (0, 1)]
    own_01, *coded = middle(at, keeps[1:], parts, beside, 0)
    coded_01, (mine_01, their_01) = coded[:3], coded[3:]
    swapped_01 = send(their_01, over_core)
    halves = fold([mine_01, mine_2], [swapped_01, swapped_2])
    coded = [jnp.concatenate([a, b]) for a, b in zip(coded_01, coded_2)]
    found = [send(coded[k - 1], over_l(k)) for k in (1, 2, 3)]
    pieces = halves.reshape(16, -1, width)
    total = jnp.sum(lax.all_to_all(pieces, ("x", "y"), 0, 0), axis=0)
    found = after(found, total)
    total = total + send(total, over_h)
    total = total + send(total, over_l(1))
    total = total + send(total, over_l(2))
    blocks = last(3, jnp.concatenate([own_01, own_2]), found)
    pieces = jnp.broadcast_to(after(total, blocks)[None], (16, *total.shape))
    mine = lax.all_to_all(pieces, ("x", "y"), 0, 0).reshape(halves.shape)
    diagonal = finish(at, mine, send(mine, over_core), diag_inverse)
    return jnp.swapaxes(blocks, 0, 1), diagonal


def solution(mesh):
    finer = Mesh(mesh.devices.reshape(SIZES), AXES)
    placed = (P(ROW, COL), P(AXES, None, None), P(), P())
    return jax.shard_map(
        body, mesh=finer, in_specs=placed, out_specs=(P(AXES, None, None), P()), check_vma=False
    )
```

```python
import functools

import jax
import jax.numpy as jnp
from jax import lax
from jax.experimental import pallas as pl
from jax.experimental.pallas import tpu as pltpu
from jax.sharding import Mesh
from jax.sharding import PartitionSpec as P

TILE = 128
AXES = ("x", "h", "core", "l", "y")
SIZES = (4, 2, 2, 4, 4)
ROW = ("x", "h", "core")
COL = ("l", "y")
EXTRA = 16
STEPS = 64.0
TOP = 32766.0
LN2 = 0.6931471805599453
VMEM = pl.BlockSpec(memory_space=pltpu.VMEM)
SMEM = pl.BlockSpec(memory_space=pltpu.SMEM)
F32, BF16, I16, I32 = jnp.float32, jnp.bfloat16, jnp.int16, jnp.int32


def coords(device):
    out = []
    for size in SIZES[::-1]:
        out.append(device % size)
        device //= size
    return tuple(out[::-1])


def number(place):
    value = 0
    for size, at in zip(SIZES, place):
        value = value * size + at
    return value


def send(value, move):
    pairs = [(d, number(move(*coords(d)))) for d in range(256)]
    return lax.ppermute(value, AXES, pairs)


def over_x(k):
    return lambda x, h, c, l, y: (x ^ k, h, c, l, y)


def over_y(k):
    return lambda x, h, c, l, y: (x, h, c, l, y ^ k)


def over_l(k):
    return lambda x, h, c, l, y: (x, h, c, l ^ k, y)


def over_h(x, h, c, l, y):
    return (x, 1 - h, c, l, y)


def over_core(x, h, c, l, y):
    return (x, h, 1 - c, l, y)


def spread(x, h, c, l, y):
    return (x ^ l, h, c, l, y)


def turn(i):
    return lambda x, h, c, l, y: (x, (y & 1) ^ i, y >> 1, x ^ l, 2 * h + c)


def params(limit=20):
    return pltpu.CompilerParams(vmem_limit_bytes=limit * 1024 * 1024)


def cost(flops, moved):
    return pl.CostEstimate(flops=flops // 1000, bytes_accessed=moved // 1000, transcendentals=0)


def diagonal_mask(rows, width):
    row = lax.broadcasted_iota(I32, (rows, width), 0)
    lane = lax.broadcasted_iota(I32, (rows, width), 1)
    return row == lane


def encode(value, out_ref, start=0):
    rows, width = value.shape
    largest = jnp.maximum(jnp.max(jnp.abs(value), axis=1, keepdims=True), 1e-30)
    level = jnp.ceil(jnp.log(largest * (1.0 / TOP)) * (STEPS / LN2))
    coded = jnp.round(value * jnp.exp2(level * (-1.0 / STEPS)))
    out_ref[start : start + rows, :] = coded.astype(I32).astype(I16)
    line = jnp.sum(jnp.where(diagonal_mask(rows, width), level, 0.0), axis=0, keepdims=True)
    lines = jnp.broadcast_to(line, (EXTRA, width))
    out_ref[start + rows : start + rows + EXTRA, :] = lines.astype(I32).astype(I16)


def decode(in_ref, start=0, rows=None):
    rows, width = rows or in_ref.shape[0] - EXTRA, in_ref.shape[1]
    coded = in_ref[start : start + rows, :].astype(I32).astype(F32)
    line = in_ref[start + rows : start + rows + EXTRA, :].astype(I32).astype(F32)[:1]
    level = jnp.sum(
        jnp.where(diagonal_mask(rows, width), jnp.broadcast_to(line, (rows, width)), 0.0),
        axis=1,
        keepdims=True,
    )
    return coded * jnp.exp2(level * (1.0 / STEPS))


def product_kernel(panels, at_ref, a_ref, own_ref, other_ref, *refs):
    outs, m_ref = refs[: 4 * panels], refs[4 * panels]
    step = pl.program_id(0)
    shard = own_ref.shape[3]

    @pl.when(step == 0)
    def _():
        core, h, t = at_ref[1], at_ref[2], at_ref[3]
        for p in range(panels):
            for k in range(4):
                for i in range(2):
                    base = (k ^ t) * (4 * shard) + (i ^ h) * shard
                    first = pl.multiple_of(base + core * (2 * shard), 32)
                    second = pl.multiple_of(base + (1 - core) * (2 * shard), 32)
                    m_ref[p, pl.ds(first, shard), :] = own_ref[k, i, p]
                    m_ref[p, pl.ds(second, shard), :] = other_ref[k, i, p]

    block = a_ref[...]
    lines = block.reshape(4 * block.shape[2], block.shape[3])
    for p in range(panels):
        value = jnp.dot(lines, m_ref[p], preferred_element_type=F32)
        for at in range(3):

            @pl.when(step == at)
            def _(ref=outs[4 * p + 1 + at], value=value):
                encode(value, ref)

        @pl.when(step == 3)
        def _(ref=outs[4 * p], value=value):
            ref[...] = value


def product(at, a4, own, other):
    shard, order = a4.shape[2], a4.shape[3]
    panels, width = own.shape[2], own.shape[4]
    rows = 4 * shard
    whole = pl.BlockSpec((4, 2, panels, shard, width), lambda g, s: (0, 0, 0, 0, 0))
    kept = pl.BlockSpec((rows, width), lambda g, s: (0, 0))
    coded = pl.BlockSpec((rows + EXTRA, width), lambda g, s: (0, 0))
    one = [jax.ShapeDtypeStruct((rows, width), F32)]
    one += [jax.ShapeDtypeStruct((rows + EXTRA, width), I16)] * 3
    outs = pl.pallas_call(
        functools.partial(product_kernel, panels),
        grid_spec=pltpu.PrefetchScalarGridSpec(
            num_scalar_prefetch=1,
            grid=(4,),
            in_specs=[
                pl.BlockSpec(
                    (4, 1, shard, order), lambda g, s: (0, s[0] ^ ((g + 1) & 3), 0, 0)
                ),
                whole,
                whole,
            ],
            out_specs=([kept] + [coded] * 3) * panels,
            scratch_shapes=[pltpu.VMEM((panels, order, width), BF16)],
        ),
        out_shape=one * panels,
        compiler_params=params(44),
        cost_estimate=cost(8 * panels * rows * order * width, 2 * order * order),
        name="product",
    )(at, a4, own, other)
    return [outs[4 * p : 4 * p + 4] for p in range(panels)]


def middle_kernel(panels, base, *refs):
    at_ref, refs = refs[0], refs[1:]
    keeps, refs = refs[:panels], refs[panels:]
    parts, refs = refs[: 3 * panels], refs[3 * panels :]
    masked, refs = refs[:4], refs[4:]
    own_ref, *coded = refs[:4]
    mine_ref, theirs_ref, sum_ref, m_ref = refs[4:]
    shard = own_ref.shape[0] // panels
    half = mine_ref.shape[0] // panels
    core, l = at_ref[1], at_ref[4]

    def place(k):
        return pl.ds(pl.multiple_of((l ^ k) * shard, 32), shard)

    for p in range(panels):
        value = keeps[p][...]
        for ref in parts[3 * p : 3 * p + 3]:
            value = value + decode(ref)
        sum_ref[...] = value
        own_ref[p * shard : (p + 1) * shard, :] = sum_ref[place(0), :]
        for k in (1, 2, 3):
            encode(sum_ref[place(k), :], coded[k - 1], p * (shard + EXTRA))
        for k, ref in enumerate(masked):
            m_ref[place(k), :] = ref[base + p]
        high = value.astype(BF16)
        rest = value - high.astype(F32)
        mid = rest.astype(BF16)
        low = (rest - mid.astype(F32)).astype(BF16)
        for which, out in ((core, mine_ref), (1 - core, theirs_ref)):
            left = m_ref[:, pl.ds(pl.multiple_of(which * half, 128), half)]
            dims = (((0,), (0,)), ((), ()))
            terms = [
                lax.dot_general(left, r, dims, preferred_element_type=F32) for r in (low, mid, high)
            ]
            out[p * half : (p + 1) * half, :] = (terms[0] + terms[1]) + terms[2]


def middle(at, keeps, parts, masked, base):
    rows, width = keeps[0].shape
    panels, shard = len(keeps), rows // 4
    return pl.pallas_call(
        functools.partial(middle_kernel, panels, base),
        in_specs=[SMEM] + [VMEM] * (4 * panels + 4),
        out_specs=[VMEM] * 6,
        out_shape=[jax.ShapeDtypeStruct((panels * shard, width), F32)]
        + [jax.ShapeDtypeStruct((panels * (shard + EXTRA), width), I16)] * 3
        + [jax.ShapeDtypeStruct((panels * (width // 2), width), F32)] * 2,
        scratch_shapes=[pltpu.VMEM((rows, width), F32), pltpu.VMEM((rows, width), BF16)],
        compiler_params=params(),
        cost_estimate=cost(6 * rows * width * width, 16 * rows * width),
        name="middle",
    )(at, *keeps, *sum(parts, []), *masked)


def last_kernel(panels, own_ref, r1_ref, r2_ref, r3_ref, out_ref):
    shard = out_ref.shape[1]
    for p in range(panels):
        total = own_ref[p * shard : (p + 1) * shard, :]
        for ref in (r1_ref, r2_ref, r3_ref):
            total = total + decode(ref, p * (shard + EXTRA), shard)
        out_ref[p] = -total


def last(panels, own, parts):
    rows, width = own.shape
    return pl.pallas_call(
        functools.partial(last_kernel, panels),
        in_specs=[VMEM] * 4,
        out_specs=VMEM,
        out_shape=jax.ShapeDtypeStruct((panels, rows // panels, width), F32),
        compiler_params=params(),
        cost_estimate=cost(8 * rows * width, 16 * rows * width),
        name="last",
    )(own, *parts)


def fold_kernel(*refs):
    out, count = refs[-1], len(refs) // 2
    start = 0
    for p in range(count):
        rows = refs[p].shape[0]
        out[start : start + rows, :] = refs[p][...] + refs[count + p][...]
        start += rows


def fold(mines, theirs):
    width = mines[0].shape[1]
    total = sum(mine.shape[0] for mine in mines)
    return pl.pallas_call(
        fold_kernel,
        in_specs=[VMEM] * (2 * len(mines)),
        out_specs=VMEM,
        out_shape=jax.ShapeDtypeStruct((total, width), F32),
        compiler_params=params(),
        cost_estimate=cost(total * width, 12 * total * width),
        name="fold",
    )(*mines, *theirs)


def finish_kernel(at_ref, mine_ref, theirs_ref, diag_ref, out_ref):
    half = diag_ref.shape[1] // 2
    core = at_ref[1]
    for p in range(diag_ref.shape[0]):
        for which, ref in ((core, mine_ref), (1 - core, theirs_ref)):
            place = pl.ds(pl.multiple_of(which * half, 8), half)
            out_ref[p, place, :] = diag_ref[p, place, :] + ref[p * half : (p + 1) * half, :]


def finish(at, mine, theirs, diag):
    return pl.pallas_call(
        finish_kernel,
        in_specs=[SMEM] + [VMEM] * 3,
        out_specs=VMEM,
        out_shape=jax.ShapeDtypeStruct(diag.shape, F32),
        compiler_params=params(),
        cost_estimate=cost(diag.size, 12 * diag.size),
        name="finish",
    )(at, mine, theirs, diag)


def after(values, *earlier):
    return lax.optimization_barrier((values, earlier))[0]


def body(ancestor_inverse, panels, diag_inverse, tile_mask):
    x, h, core, l, y = (lax.axis_index(axis) for axis in AXES)
    at = jnp.stack([y, core, h, x ^ l, l, x]).astype(I32)
    kept, count, width = panels.shape
    order = ancestor_inverse.shape[1]
    tiles = tile_mask.shape[1]
    start = (((x * 2 + h) * 2 + core) * 16 + l * 4 + y) * kept
    tile = start // TILE
    first = lax.dynamic_slice_in_dim(tile_mask, tile, 1, 1)
    second = lax.dynamic_slice_in_dim(tile_mask, jnp.minimum(tile + 1, tiles - 1), 1, 1)
    in_first = start + jnp.arange(kept) < (tile + 1) * TILE
    own_mask = jnp.where(in_first[None, :], first, second).astype(BF16)
    masked = jnp.swapaxes(panels, 0, 1) * own_mask[:, :, None]

    def gather(message):
        return [message] + [send(message, over_x(k)) for k in (1, 2, 3)]

    a4 = ancestor_inverse.reshape(4, 4, kept, order)
    moved_a, moved_b = send(masked[2:], spread), send(masked[:2], spread)
    turned_a = [send(moved_a, turn(i)) for i in range(2)]
    turned_b = [send(moved_b, turn(i)) for i in range(2)]
    own_a = gather(after(jnp.stack(turned_a), moved_b))
    own_a = after(jnp.stack(own_a), turned_b)
    own_b = gather(after(jnp.stack(turned_b), own_a))
    ((keep_a, *coded),) = product(at, a4, own_a, send(own_a, over_core))
    parts_a = [send(coded[k - 1], over_y(k)) for k in (1, 2, 3)]
    own_b = after(jnp.stack(own_b), parts_a[0], parts_a[2])
    outs = product(at, a4, own_b, send(own_b, over_core))
    late = after(masked, own_b)
    beside = [masked] + [send(late, over_l(k)) for k in (1, 2, 3)]
    pairs = [jnp.stack([outs[0][k], outs[1][k]]) for k in (1, 2, 3)]
    pairs = after(pairs, parts_a)
    pairs = [send(pairs[k - 1], over_y(k)) for k in (1, 2, 3)]
    keeps, parts = [keep_a, outs[0][0], outs[1][0]], [parts_a]
    own_2, *coded = middle(at, keeps[:1], parts[:1], beside, 2)
    coded_2, (mine_2, their_2) = coded[:3], coded[3:]
    swapped_2 = send(their_2, over_core)
    pairs = after(pairs, mine_2)
    parts = [[pair[p] for pair in pairs] for p in (0, 1)]
    own_01, *coded = middle(at, keeps[1:], parts, beside, 0)
    coded_01, (mine_01, their_01) = coded[:3], coded[3:]
    swapped_01 = send(their_01, over_core)
    halves = fold([mine_01, mine_2], [swapped_01, swapped_2])
    coded = [jnp.concatenate([a, b]) for a, b in zip(coded_01, coded_2)]
    found = [send(coded[k - 1], over_l(k)) for k in (1, 2, 3)]
    pieces = halves.reshape(16, -1, width)
    total = jnp.sum(lax.all_to_all(pieces, ("x", "y"), 0, 0), axis=0)
    found = after(found, total)
    total = total + send(total, over_h)
    total = total + send(total, over_l(1))
    total = total + send(total, over_l(2))
    blocks = last(3, jnp.concatenate([own_01, own_2]), found)
    pieces = jnp.broadcast_to(after(total, blocks)[None], (16, *total.shape))
    mine = lax.all_to_all(pieces, ("x", "y"), 0, 0).reshape(halves.shape)
    diagonal = finish(at, mine, send(mine, over_core), diag_inverse)
    return jnp.swapaxes(blocks, 0, 1), diagonal


def solution(mesh):
    finer = Mesh(mesh.devices.reshape(SIZES), AXES)
    placed = (P(ROW, COL), P(AXES, None, None), P(), P())
    return jax.shard_map(
        body, mesh=finer, in_specs=placed, out_specs=(P(AXES, None, None), P()), check_vma=False
    )
```

```python
import functools

import jax
import jax.numpy as jnp
from jax import lax
from jax.experimental import pallas as pl
from jax.experimental.pallas import tpu as pltpu
from jax.sharding import Mesh
from jax.sharding import PartitionSpec as P

TILE = 128
AXES = ("x", "h", "core", "l", "y")
SIZES = (4, 2, 2, 4, 4)
ROW = ("x", "h", "core")
COL = ("l", "y")
EXTRA = 16
STEPS = 64.0
TOP = 32766.0
LN2 = 0.6931471805599453
VMEM = pl.BlockSpec(memory_space=pltpu.VMEM)
SMEM = pl.BlockSpec(memory_space=pltpu.SMEM)
F32, BF16, I16, I32 = jnp.float32, jnp.bfloat16, jnp.int16, jnp.int32


def coords(device):
    out = []
    for size in SIZES[::-1]:
        out.append(device % size)
        device //= size
    return tuple(out[::-1])


def number(place):
    value = 0
    for size, at in zip(SIZES, place):
        value = value * size + at
    return value


def send(value, move):
    pairs = [(d, number(move(*coords(d)))) for d in range(256)]
    return lax.ppermute(value, AXES, pairs)


def over_x(k):
    return lambda x, h, c, l, y: (x ^ k, h, c, l, y)


def over_y(k):
    return lambda x, h, c, l, y: (x, h, c, l, y ^ k)


def over_l(k):
    return lambda x, h, c, l, y: (x, h, c, l ^ k, y)


def over_h(x, h, c, l, y):
    return (x, 1 - h, c, l, y)


def over_core(x, h, c, l, y):
    return (x, h, 1 - c, l, y)


def spread(x, h, c, l, y):
    return (x ^ l, h, c, l, y)


def turn(i):
    return lambda x, h, c, l, y: (x, (y & 1) ^ i, y >> 1, x ^ l, 2 * h + c)


def params(limit=16):
    return pltpu.CompilerParams(vmem_limit_bytes=limit * 1024 * 1024)


def cost(flops, moved):
    return pl.CostEstimate(flops=flops // 1000, bytes_accessed=moved // 1000, transcendentals=0)


def diagonal_mask(rows, width):
    row = lax.broadcasted_iota(I32, (rows, width), 0)
    lane = lax.broadcasted_iota(I32, (rows, width), 1)
    return row == lane


def encode(value, out_ref, start=0):
    rows, width = value.shape
    largest = jnp.maximum(jnp.max(jnp.abs(value), axis=1, keepdims=True), 1e-30)
    level = jnp.ceil(jnp.log(largest * (1.0 / TOP)) * (STEPS / LN2))
    coded = jnp.round(value * jnp.exp2(level * (-1.0 / STEPS)))
    out_ref[start : start + rows, :] = coded.astype(I32).astype(I16)
    line = jnp.sum(jnp.where(diagonal_mask(rows, width), level, 0.0), axis=0, keepdims=True)
    lines = jnp.broadcast_to(line, (EXTRA, width))
    out_ref[start + rows : start + rows + EXTRA, :] = lines.astype(I32).astype(I16)


def decode(in_ref, start=0, rows=None):
    rows, width = rows or in_ref.shape[0] - EXTRA, in_ref.shape[1]
    coded = in_ref[start : start + rows, :].astype(I32).astype(F32)
    line = in_ref[start + rows : start + rows + EXTRA, :].astype(I32).astype(F32)[:1]
    level = jnp.sum(
        jnp.where(diagonal_mask(rows, width), jnp.broadcast_to(line, (rows, width)), 0.0),
        axis=1,
        keepdims=True,
    )
    return coded * jnp.exp2(level * (1.0 / STEPS))


def product_kernel(at_ref, a_ref, own_ref, other_ref, keep_ref, q_ref, m_ref):
    step = pl.program_id(0)
    shard = own_ref.shape[3]

    @pl.when(step == 0)
    def _():
        core, h, t = at_ref[1], at_ref[2], at_ref[3]
        for k in range(4):
            for i in range(2):
                base = (k ^ t) * (4 * shard) + (i ^ h) * shard
                first = pl.multiple_of(base + core * (2 * shard), 32)
                second = pl.multiple_of(base + (1 - core) * (2 * shard), 32)
                m_ref[pl.ds(first, shard), :] = own_ref[k, i, 0]
                m_ref[pl.ds(second, shard), :] = other_ref[k, i, 0]

    block = a_ref[...]
    lines = block.reshape(4 * block.shape[2], block.shape[3])
    value = jnp.dot(lines, m_ref[...], preferred_element_type=F32)
    encode(value, q_ref.at[at_ref[0] ^ ((step + 1) & 3)])

    @pl.when(step == 3)
    def _():
        keep_ref[...] = value


def product(at, a4, own, other, first=0):
    shard, order = a4.shape[2], a4.shape[3]
    width = own.shape[4]
    rows = 4 * shard
    whole = pl.BlockSpec((4, 2, 1, shard, width), lambda g, s: (0, 0, first, 0, 0))
    return pl.pallas_call(
        product_kernel,
        grid_spec=pltpu.PrefetchScalarGridSpec(
            num_scalar_prefetch=1,
            grid=(4,),
            in_specs=[
                pl.BlockSpec(
                    (4, 1, shard, order), lambda g, s: (0, s[0] ^ ((g + 1) & 3), 0, 0)
                ),
                whole,
                whole,
            ],
            out_specs=[
                pl.BlockSpec((rows, width), lambda g, s: (0, 0)),
                pl.BlockSpec((4, rows + EXTRA, width), lambda g, s: (0, 0, 0)),
            ],
            scratch_shapes=[pltpu.VMEM((order, width), BF16)],
        ),
        out_shape=[
            jax.ShapeDtypeStruct((rows, width), F32),
            jax.ShapeDtypeStruct((4, rows + EXTRA, width), I16),
        ],
        compiler_params=params(20),
        cost_estimate=cost(8 * rows * order * width, 2 * order * order),
        name="product",
    )(at, a4, own, other)


def middle_kernel(panels, which, *refs):
    at_ref, refs = refs[0], refs[1:]
    keeps, parts, refs = refs[:panels], refs[panels : 2 * panels], refs[2 * panels :]
    masked, refs = refs[:4], refs[4:]
    own_ref, *coded = refs[:4]
    mine_ref, theirs_ref, sum_ref, m_ref = refs[4:]
    shard = own_ref.shape[0] // panels
    half = mine_ref.shape[0] // panels
    y, core, l = at_ref[0], at_ref[1], at_ref[4]
    for p in range(panels):
        value = keeps[p][...]
        for k in (1, 2, 3):
            value = value + decode(parts[p].at[y ^ k])
        sum_ref[...] = value
        for k in range(4):
            place = pl.ds(pl.multiple_of((l ^ k) * shard, 32), shard)
            part = sum_ref[place, :]
            if k:
                encode(part, coded[k - 1], p * (shard + EXTRA))
            else:
                own_ref[p * shard : (p + 1) * shard, :] = part
            m_ref[place, :] = masked[k][which[p]]
        high = value.astype(BF16)
        rest = value - high.astype(F32)
        mid = rest.astype(BF16)
        low = (rest - mid.astype(F32)).astype(BF16)
        for side, out in ((core, mine_ref), (1 - core, theirs_ref)):
            left = m_ref[:, pl.ds(pl.multiple_of(side * half, 128), half)]
            dims = (((0,), (0,)), ((), ()))
            terms = [
                lax.dot_general(left, r, dims, preferred_element_type=F32) for r in (low, mid, high)
            ]
            out[p * half : (p + 1) * half, :] = (terms[0] + terms[1]) + terms[2]


def middle(at, keeps, parts, masked, which):
    rows, width = keeps[0].shape
    panels, shard = len(keeps), rows // 4
    return pl.pallas_call(
        functools.partial(middle_kernel, panels, which),
        in_specs=[SMEM] + [VMEM] * (2 * panels + 4),
        out_specs=[VMEM] * 6,
        out_shape=[jax.ShapeDtypeStruct((panels * shard, width), F32)]
        + [jax.ShapeDtypeStruct((panels * (shard + EXTRA), width), I16)] * 3
        + [jax.ShapeDtypeStruct((panels * (width // 2), width), F32)] * 2,
        scratch_shapes=[pltpu.VMEM((rows, width), F32), pltpu.VMEM((rows, width), BF16)],
        compiler_params=params(),
        cost_estimate=cost(6 * rows * width * width, 16 * rows * width),
        name="middle",
    )(at, *keeps, *parts, *masked)


def last_kernel(groups, *refs):
    out_ref = refs[-1]
    shard = out_ref.shape[1]
    for g, which in enumerate(groups):
        own_ref, *parts = refs[4 * g : 4 * g + 4]
        for p, panel in enumerate(which):
            total = own_ref[p * shard : (p + 1) * shard, :]
            for ref in parts:
                total = total + decode(ref, p * (shard + EXTRA), shard)
            out_ref[panel] = -total


def last(groups, shape):
    ins = [ref for own, parts, _ in groups for ref in (own, *parts)]
    return pl.pallas_call(
        functools.partial(last_kernel, [which for _, _, which in groups]),
        in_specs=[VMEM] * len(ins),
        out_specs=VMEM,
        out_shape=jax.ShapeDtypeStruct(shape, F32),
        compiler_params=params(),
        cost_estimate=cost(8 * shape[1] * shape[2], 16 * shape[1] * shape[2]),
        name="last",
    )(*ins)


def fold_kernel(*refs):
    out, count = refs[-1], len(refs) // 2
    start = 0
    for p in range(count):
        rows = refs[p].shape[0]
        out[start : start + rows, :] = refs[p][...] + refs[count + p][...]
        start += rows


def fold(mines, theirs):
    width = mines[0].shape[1]
    total = sum(mine.shape[0] for mine in mines)
    return pl.pallas_call(
        fold_kernel,
        in_specs=[VMEM] * (2 * len(mines)),
        out_specs=VMEM,
        out_shape=jax.ShapeDtypeStruct((total, width), F32),
        compiler_params=params(),
        cost_estimate=cost(total * width, 12 * total * width),
        name="fold",
    )(*mines, *theirs)


def finish_kernel(at_ref, mine_ref, theirs_ref, diag_ref, out_ref):
    half = diag_ref.shape[1] // 2
    core = at_ref[1]
    for at, p in enumerate((0, 2, 1)):
        for side, ref in ((core, mine_ref), (1 - core, theirs_ref)):
            place = pl.ds(pl.multiple_of(side * half, 8), half)
            out_ref[p, place, :] = diag_ref[p, place, :] + ref[at * half : (at + 1) * half, :]


def finish(at, mine, theirs, diag):
    return pl.pallas_call(
        finish_kernel,
        in_specs=[SMEM] + [VMEM] * 3,
        out_specs=VMEM,
        out_shape=jax.ShapeDtypeStruct(diag.shape, F32),
        compiler_params=params(),
        cost_estimate=cost(diag.size, 12 * diag.size),
        name="finish",
    )(at, mine, theirs, diag)


def after(values, *earlier):
    return lax.optimization_barrier((values, earlier))[0]


def body(ancestor_inverse, panels, diag_inverse, tile_mask):
    x, h, core, l, y = (lax.axis_index(axis) for axis in AXES)
    at = jnp.stack([y, core, h, x ^ l, l, x]).astype(I32)
    kept, count, width = panels.shape
    order = ancestor_inverse.shape[1]
    tiles = tile_mask.shape[1]
    start = (((x * 2 + h) * 2 + core) * 16 + l * 4 + y) * kept
    tile = start // TILE
    first = lax.dynamic_slice_in_dim(tile_mask, tile, 1, 1)
    second = lax.dynamic_slice_in_dim(tile_mask, jnp.minimum(tile + 1, tiles - 1), 1, 1)
    in_first = start + jnp.arange(kept) < (tile + 1) * TILE
    own_mask = jnp.where(in_first[None, :], first, second).astype(BF16)
    masked = jnp.swapaxes(panels, 0, 1) * own_mask[:, :, None]

    def gather(message):
        return [message] + [send(message, over_x(k)) for k in (1, 2, 3)]

    def exchange(value, axis):
        return lax.all_to_all(value, axis, 0, 0)

    a4 = ancestor_inverse.reshape(4, 4, kept, order)
    moved_a, moved_b = send(masked[2:], spread), send(masked[:2], spread)
    turned_a = [send(moved_a, turn(i)) for i in range(2)]
    turned_b = [send(moved_b, turn(i)) for i in range(2)]
    own_a = gather(after(jnp.stack(turned_a), moved_b))
    own_a = after(jnp.stack(own_a), turned_b)
    own_b = gather(after(jnp.stack(turned_b), own_a))
    late = after(masked, own_a)
    beside = [masked] + [send(late, over_l(k)) for k in (1, 2, 3)]
    keep_a, coded = product(at, a4, own_a, send(own_a, over_core))
    part_a = exchange(coded, "y")
    own_b = jnp.stack(after(own_b, keep_a, beside[2]))
    other_b = send(own_b, over_core)
    keep_b, coded = product(after(at, beside[1], beside[3]), a4, own_b, other_b, 0)
    part_b = exchange(coded, "y")
    keep_c, coded = product(at, a4, own_b, other_b, 1)
    part_c = exchange(coded, "y")
    own_ab, *coded = middle(at, [keep_b, keep_a], [part_b, part_a], beside, (0, 2))
    coded_ab, (mine_ab, their_ab) = coded[:3], coded[3:]
    swapped_ab = send(their_ab, over_core)
    found_ab = [send(coded_ab[k - 1], over_l(k)) for k in (1, 2, 3)]
    part_c = after(part_c, found_ab)
    own_c, *coded = middle(at, [keep_c], [part_c], beside, (1,))
    coded_c, (mine_c, their_c) = coded[:3], coded[3:]
    halves = fold([mine_ab, mine_c], [swapped_ab, send(their_c, over_core)])
    found_c = [send(coded_c[k - 1], over_l(k)) for k in (1, 2, 3)]
    total = jnp.sum(exchange(halves.reshape(16, -1, width), ("x", "y")), axis=0)
    found_c = after(found_c, total)
    total = total + send(total, over_h)
    total = total + send(total, over_l(1))
    total = total + send(total, over_l(2))
    blocks = last([(own_ab, found_ab, (0, 2)), (own_c, found_c, (1,))], masked.shape)
    pieces = jnp.broadcast_to(after(total, blocks)[None], (16, *total.shape))
    mine = exchange(pieces, ("x", "y")).reshape(halves.shape)
    diagonal = finish(at, mine, send(mine, over_core), diag_inverse)
    return jnp.swapaxes(blocks, 0, 1), diagonal


def solution(mesh):
    finer = Mesh(mesh.devices.reshape(SIZES), AXES)
    placed = (P(ROW, COL), P(AXES, None, None), P(), P())
    return jax.shard_map(
        body, mesh=finer, in_specs=placed, out_specs=(P(AXES, None, None), P()), check_vma=False
    )
```

```python
import functools

import jax
import jax.numpy as jnp
from jax import lax
from jax.experimental import pallas as pl
from jax.experimental.pallas import tpu as pltpu
from jax.sharding import Mesh
from jax.sharding import PartitionSpec as P

TILE = 128
AXES = ("x", "h", "core", "l", "y")
SIZES = (4, 2, 2, 4, 4)
ROW = ("x", "h", "core")
COL = ("l", "y")
EXTRA = 16
LANES = 128
STEPS = 64.0
TOP = 32766.0
LN2 = 0.6931471805599453
VMEM = pl.BlockSpec(memory_space=pltpu.VMEM)
SMEM = pl.BlockSpec(memory_space=pltpu.SMEM)
F32, BF16, I16, I32 = jnp.float32, jnp.bfloat16, jnp.int16, jnp.int32


def coords(device):
    out = []
    for size in SIZES[::-1]:
        out.append(device % size)
        device //= size
    return tuple(out[::-1])


def number(place):
    value = 0
    for size, at in zip(SIZES, place):
        value = value * size + at
    return value


def send(value, move):
    pairs = [(d, number(move(*coords(d)))) for d in range(256)]
    return lax.ppermute(value, AXES, pairs)


def over_x(k):
    return lambda x, h, c, l, y: (x ^ k, h, c, l, y)


def over_y(k):
    return lambda x, h, c, l, y: (x, h, c, l, y ^ k)


def over_l(k):
    return lambda x, h, c, l, y: (x, h, c, l ^ k, y)


def over_h(x, h, c, l, y):
    return (x, 1 - h, c, l, y)


def over_core(x, h, c, l, y):
    return (x, h, 1 - c, l, y)


def spread(x, h, c, l, y):
    return (x ^ l, h, c, l, y)


def turn(i):
    return lambda x, h, c, l, y: (x, (y & 1) ^ i, y >> 1, x ^ l, 2 * h + c)


def params(limit=20):
    return pltpu.CompilerParams(vmem_limit_bytes=limit * 1024 * 1024)


def cost(flops, moved):
    return pl.CostEstimate(flops=flops // 1000, bytes_accessed=moved // 1000, transcendentals=0)


def diagonal_mask(rows, width):
    row = lax.broadcasted_iota(I32, (rows, width), 0)
    lane = lax.broadcasted_iota(I32, (rows, width), 1)
    return row == lane


def encode(value, out_ref, start=0):
    rows, width = value.shape
    largest = jnp.maximum(jnp.max(jnp.abs(value), axis=1, keepdims=True), 1e-30)
    level = jnp.ceil(jnp.log(largest * (1.0 / TOP)) * (STEPS / LN2))
    coded = jnp.round(value * jnp.exp2(level * (-1.0 / STEPS)))
    out_ref[start : start + rows, :] = coded.astype(I32).astype(I16)
    line = jnp.sum(jnp.where(diagonal_mask(rows, width), level, 0.0), axis=0, keepdims=True)
    lines = jnp.broadcast_to(line, (EXTRA, width))
    out_ref[start + rows : start + rows + EXTRA, :] = lines.astype(I32).astype(I16)


def decode(in_ref, start=0, rows=None):
    rows, width = rows or in_ref.shape[0] - EXTRA, in_ref.shape[1]
    coded = in_ref[start : start + rows, :].astype(I32).astype(F32)
    line = in_ref[start + rows : start + rows + EXTRA, :].astype(I32).astype(F32)[:1]
    level = jnp.sum(
        jnp.where(diagonal_mask(rows, width), jnp.broadcast_to(line, (rows, width)), 0.0),
        axis=1,
        keepdims=True,
    )
    return coded * jnp.exp2(level * (1.0 / STEPS))


def product_kernel(panels, at_ref, a_ref, own_ref, other_ref, *refs):
    outs, m_ref = refs[: 4 * panels], refs[4 * panels]
    step = pl.program_id(0)
    shard = own_ref.shape[3]

    @pl.when(step == 0)
    def _():
        core, h, t = at_ref[1], at_ref[2], at_ref[3]
        for p in range(panels):
            for k in range(4):
                for i in range(2):
                    base = (k ^ t) * (4 * shard) + (i ^ h) * shard
                    first = pl.multiple_of(base + core * (2 * shard), 32)
                    second = pl.multiple_of(base + (1 - core) * (2 * shard), 32)
                    m_ref[p, pl.ds(first, shard), :] = own_ref[k, i, p]
                    m_ref[p, pl.ds(second, shard), :] = other_ref[k, i, p]

    block = a_ref[...]
    lines = block.reshape(4 * block.shape[2], block.shape[3])
    for p in range(panels):
        value = jnp.dot(lines, m_ref[p], preferred_element_type=F32)
        for at in range(3):

            @pl.when(step == at)
            def _(ref=outs[4 * p + 1 + at], value=value):
                encode(value, ref)

        @pl.when(step == 3)
        def _(ref=outs[4 * p], value=value):
            ref[...] = value


def product(at, a4, own, other):
    shard, order = a4.shape[2], a4.shape[3]
    panels, width = own.shape[2], own.shape[4]
    rows = 4 * shard
    whole = pl.BlockSpec((4, 2, panels, shard, width), lambda g, s: (0, 0, 0, 0, 0))
    kept = pl.BlockSpec((rows, width), lambda g, s: (0, 0))
    coded = pl.BlockSpec((rows + EXTRA, width), lambda g, s: (0, 0))
    one = [jax.ShapeDtypeStruct((rows, width), F32)]
    one += [jax.ShapeDtypeStruct((rows + EXTRA, width), I16)] * 3
    outs = pl.pallas_call(
        functools.partial(product_kernel, panels),
        grid_spec=pltpu.PrefetchScalarGridSpec(
            num_scalar_prefetch=1,
            grid=(4,),
            in_specs=[
                pl.BlockSpec(
                    (4, 1, shard, order), lambda g, s: (0, s[0] ^ ((g + 1) & 3), 0, 0)
                ),
                whole,
                whole,
            ],
            out_specs=([kept] + [coded] * 3) * panels,
            scratch_shapes=[pltpu.VMEM((panels, order, width), BF16)],
        ),
        out_shape=one * panels,
        compiler_params=params(44),
        cost_estimate=cost(8 * panels * rows * order * width, 2 * order * order),
        name="product",
    )(at, a4, own, other)
    return [outs[4 * p : 4 * p + 4] for p in range(panels)]


def middle_kernel(panels, base, *refs):
    at_ref, refs = refs[0], refs[1:]
    keeps, refs = refs[:panels], refs[panels:]
    parts, refs = refs[: 3 * panels], refs[3 * panels :]
    masked, refs = refs[:4], refs[4:]
    own_ref, *coded = refs[:4]
    mine_ref, theirs_ref, sum_ref, m_ref = refs[4:]
    shard = own_ref.shape[0] // panels
    half = mine_ref.shape[0] // panels
    core, l = at_ref[1], at_ref[4]

    def place(k):
        return pl.ds(pl.multiple_of((l ^ k) * shard, 32), shard)

    for p in range(panels):
        value = keeps[p][...]
        for ref in parts[3 * p : 3 * p + 3]:
            value = value + decode(ref)
        sum_ref[...] = value
        own_ref[p * shard : (p + 1) * shard, :] = sum_ref[place(0), :]
        for k in (1, 2, 3):
            encode(sum_ref[place(k), :], coded[k - 1], p * (shard + EXTRA))
        for k, ref in enumerate(masked):
            m_ref[place(k), :] = ref[base + p]
        high = value.astype(BF16)
        rest = value - high.astype(F32)
        mid = rest.astype(BF16)
        low = (rest - mid.astype(F32)).astype(BF16)
        for which, out in ((core, mine_ref), (1 - core, theirs_ref)):
            left = m_ref[:, pl.ds(pl.multiple_of(which * half, 128), half)]
            dims = (((0,), (0,)), ((), ()))
            terms = [
                lax.dot_general(left, r, dims, preferred_element_type=F32) for r in (low, mid, high)
            ]
            out[p * half : (p + 1) * half, :] = (terms[0] + terms[1]) + terms[2]


def middle(at, keeps, parts, masked, base):
    rows, width = keeps[0].shape
    panels, shard = len(keeps), rows // 4
    return pl.pallas_call(
        functools.partial(middle_kernel, panels, base),
        in_specs=[SMEM] + [VMEM] * (4 * panels + 4),
        out_specs=[VMEM] * 6,
        out_shape=[jax.ShapeDtypeStruct((panels * shard, width), F32)]
        + [jax.ShapeDtypeStruct((panels * (shard + EXTRA), width), I16)] * 3
        + [jax.ShapeDtypeStruct((panels * (width // 2), width), F32)] * 2,
        scratch_shapes=[pltpu.VMEM((rows, width), F32), pltpu.VMEM((rows, width), BF16)],
        compiler_params=params(),
        cost_estimate=cost(6 * rows * width * width, 16 * rows * width),
        name="middle",
    )(at, *keeps, *sum(parts, []), *masked)


def last_kernel(panels, own_ref, r1_ref, r2_ref, r3_ref, out_ref):
    shard = out_ref.shape[1]
    for p in range(panels):
        total = own_ref[p * shard : (p + 1) * shard, :]
        for ref in (r1_ref, r2_ref, r3_ref):
            total = total + decode(ref, p * (shard + EXTRA), shard)
        out_ref[p] = -total


def last(panels, own, parts):
    rows, width = own.shape
    return pl.pallas_call(
        functools.partial(last_kernel, panels),
        in_specs=[VMEM] * 4,
        out_specs=VMEM,
        out_shape=jax.ShapeDtypeStruct((panels, rows // panels, width), F32),
        compiler_params=params(),
        cost_estimate=cost(8 * rows * width, 16 * rows * width),
        name="last",
    )(own, *parts)


def encode_lanes(value, out_ref, start=0):
    rows, width = value.shape
    largest = jnp.maximum(jnp.max(jnp.abs(value), axis=1, keepdims=True), 1e-30)
    level = jnp.ceil(jnp.log(largest * (1.0 / TOP)) * (STEPS / LN2))
    coded = jnp.round(value * jnp.exp2(level * (-1.0 / STEPS)))
    out_ref[start : start + rows, :width] = coded.astype(I32).astype(I16)
    lanes = jnp.broadcast_to(level, (rows, LANES))
    out_ref[start : start + rows, width:] = lanes.astype(I32).astype(I16)


def decode_lanes(block):
    width = block.shape[1] - LANES
    coded = block[:, :width].astype(I32).astype(F32)
    level = block[:, width:].astype(I32).astype(F32)[:, :1]
    return coded * jnp.exp2(level * (1.0 / STEPS))


def fold_kernel(*refs):
    out, count = refs[-1], len(refs) // 2
    start = 0
    for p in range(count):
        rows = refs[p].shape[0]
        encode_lanes(refs[p][...] + refs[count + p][...], out, start)
        start += rows


def fold(mines, theirs):
    width = mines[0].shape[1]
    total = sum(mine.shape[0] for mine in mines)
    return pl.pallas_call(
        fold_kernel,
        in_specs=[VMEM] * (2 * len(mines)),
        out_specs=VMEM,
        out_shape=jax.ShapeDtypeStruct((total, width + LANES), I16),
        compiler_params=params(),
        cost_estimate=cost(total * width, 12 * total * width),
        name="fold",
    )(*mines, *theirs)


def gathered_kernel(in_ref, out_ref):
    total = decode_lanes(in_ref[0])
    for k in range(1, in_ref.shape[0]):
        total = total + decode_lanes(in_ref[k])
    out_ref[...] = total


def gathered(pieces):
    count, rows, lanes = pieces.shape
    return pl.pallas_call(
        gathered_kernel,
        in_specs=[VMEM],
        out_specs=VMEM,
        out_shape=jax.ShapeDtypeStruct((rows, lanes - LANES), F32),
        compiler_params=params(),
        cost_estimate=cost(count * rows * lanes, 2 * count * rows * lanes),
        name="gathered",
    )(pieces)


def copies_kernel(own_ref, r1_ref, r2_ref, r3_ref, out_ref):
    total = (own_ref[...] + r1_ref[...]) + (r2_ref[...] + r3_ref[...])
    encode_lanes(total, out_ref.at[0])
    for k in range(1, out_ref.shape[0]):
        out_ref[k] = out_ref[0]


def copies(own, found):
    rows, width = own.shape
    return pl.pallas_call(
        copies_kernel,
        in_specs=[VMEM] * 4,
        out_specs=VMEM,
        out_shape=jax.ShapeDtypeStruct((16, rows, width + LANES), I16),
        compiler_params=params(),
        cost_estimate=cost(rows * width, 32 * rows * width),
        name="copies",
    )(own, *found)


def finish_kernel(at_ref, mine_ref, theirs_ref, diag_ref, out_ref):
    half = diag_ref.shape[1] // 2
    core = at_ref[1]
    for p in range(diag_ref.shape[0]):
        for which, ref in ((core, mine_ref), (1 - core, theirs_ref)):
            place = pl.ds(pl.multiple_of(which * half, 8), half)
            part = decode_lanes(ref[p * half : (p + 1) * half, :])
            out_ref[p, place, :] = diag_ref[p, place, :] + part


def finish(at, mine, theirs, diag):
    return pl.pallas_call(
        finish_kernel,
        in_specs=[SMEM] + [VMEM] * 3,
        out_specs=VMEM,
        out_shape=jax.ShapeDtypeStruct(diag.shape, F32),
        compiler_params=params(),
        cost_estimate=cost(diag.size, 12 * diag.size),
        name="finish",
    )(at, mine, theirs, diag)


def after(values, *earlier):
    return lax.optimization_barrier((values, earlier))[0]


def body(ancestor_inverse, panels, diag_inverse, tile_mask):
    x, h, core, l, y = (lax.axis_index(axis) for axis in AXES)
    at = jnp.stack([y, core, h, x ^ l, l, x]).astype(I32)
    kept, count, width = panels.shape
    order = ancestor_inverse.shape[1]
    tiles = tile_mask.shape[1]
    start = (((x * 2 + h) * 2 + core) * 16 + l * 4 + y) * kept
    tile = start // TILE
    first = lax.dynamic_slice_in_dim(tile_mask, tile, 1, 1)
    second = lax.dynamic_slice_in_dim(tile_mask, jnp.minimum(tile + 1, tiles - 1), 1, 1)
    in_first = start + jnp.arange(kept) < (tile + 1) * TILE
    own_mask = jnp.where(in_first[None, :], first, second).astype(BF16)
    masked = jnp.swapaxes(panels, 0, 1) * own_mask[:, :, None]

    def gather(message):
        return [message] + [send(message, over_x(k)) for k in (1, 2, 3)]

    a4 = ancestor_inverse.reshape(4, 4, kept, order)
    moved_a, moved_b = send(masked[2:], spread), send(masked[:2], spread)
    turned_a = [send(moved_a, turn(i)) for i in range(2)]
    turned_b = [send(moved_b, turn(i)) for i in range(2)]
    own_a = gather(after(jnp.stack(turned_a), moved_b))
    own_a = after(jnp.stack(own_a), turned_b)
    own_b = gather(after(jnp.stack(turned_b), own_a))
    ((keep_a, *coded),) = product(at, a4, own_a, send(own_a, over_core))
    parts_a = [send(coded[k - 1], over_y(k)) for k in (1, 2, 3)]
    own_b = after(jnp.stack(own_b), parts_a[0], parts_a[2])
    outs = product(at, a4, own_b, send(own_b, over_core))
    late = after(masked, own_b)
    beside = [masked] + [send(late, over_l(k)) for k in (1, 2, 3)]
    pairs = [jnp.stack([outs[0][k], outs[1][k]]) for k in (1, 2, 3)]
    pairs = after(pairs, parts_a)
    pairs = [send(pairs[k - 1], over_y(k)) for k in (1, 2, 3)]
    keeps, parts = [keep_a, outs[0][0], outs[1][0]], [parts_a]
    own_2, *coded = middle(at, keeps[:1], parts[:1], beside, 2)
    coded_2, (mine_2, their_2) = coded[:3], coded[3:]
    swapped_2 = send(their_2, over_core)
    pairs = after(pairs, mine_2)
    parts = [[pair[p] for pair in pairs] for p in (0, 1)]
    own_01, *coded = middle(at, keeps[1:], parts, beside, 0)
    coded_01, (mine_01, their_01) = coded[:3], coded[3:]
    swapped_01 = send(their_01, over_core)
    halves = fold([mine_01, mine_2], [swapped_01, swapped_2])
    coded = [jnp.concatenate([a, b]) for a, b in zip(coded_01, coded_2)]
    found = [send(coded[k - 1], over_l(k)) for k in (1, 2, 3)]
    pieces = halves.reshape(16, -1, width + LANES)
    total = gathered(lax.all_to_all(pieces, ("x", "y"), 0, 0))
    found = after(found, total)
    total = total + send(total, over_h)
    beyond = [send(total, over_l(k)) for k in (1, 2, 3)]
    blocks = last(3, jnp.concatenate([own_01, own_2]), found)
    pieces = copies(total, after(beyond, blocks))
    mine = lax.all_to_all(pieces, ("x", "y"), 0, 0).reshape(halves.shape)
    diagonal = finish(at, mine, send(mine, over_core), diag_inverse)
    return jnp.swapaxes(blocks, 0, 1), diagonal


def solution(mesh):
    finer = Mesh(mesh.devices.reshape(SIZES), AXES)
    placed = (P(ROW, COL), P(AXES, None, None), P(), P())
    return jax.shard_map(
        body, mesh=finer, in_specs=placed, out_specs=(P(AXES, None, None), P()), check_vma=False
    )
```

```python
import functools

import jax
import jax.numpy as jnp
from jax import lax
from jax.experimental import pallas as pl
from jax.experimental.pallas import tpu as pltpu
from jax.sharding import Mesh
from jax.sharding import PartitionSpec as P

TILE = 128
AXES = ("x", "h", "core", "l", "y")
SIZES = (4, 2, 2, 4, 4)
ROW = ("x", "h", "core")
COL = ("l", "y")
EXTRA = 16
LANES = 128
STEPS = 64.0
TOP = 32766.0
LN2 = 0.6931471805599453
VMEM = pl.BlockSpec(memory_space=pltpu.VMEM)
SMEM = pl.BlockSpec(memory_space=pltpu.SMEM)
F32, BF16, I16, I32 = jnp.float32, jnp.bfloat16, jnp.int16, jnp.int32


def coords(device):
    out = []
    for size in SIZES[::-1]:
        out.append(device % size)
        device //= size
    return tuple(out[::-1])


def number(place):
    value = 0
    for size, at in zip(SIZES, place):
        value = value * size + at
    return value


def send(value, move):
    pairs = [(d, number(move(*coords(d)))) for d in range(256)]
    return lax.ppermute(value, AXES, pairs)


def over_x(k):
    return lambda x, h, c, l, y: (x ^ k, h, c, l, y)


def over_y(k):
    return lambda x, h, c, l, y: (x, h, c, l, y ^ k)


def over_l(k):
    return lambda x, h, c, l, y: (x, h, c, l ^ k, y)


def over_h(x, h, c, l, y):
    return (x, 1 - h, c, l, y)


def over_core(x, h, c, l, y):
    return (x, h, 1 - c, l, y)


def spread(x, h, c, l, y):
    return (x ^ l, h, c, l, y)


def turn(i):
    return lambda x, h, c, l, y: (x, (y & 1) ^ i, y >> 1, x ^ l, 2 * h + c)


def params(limit=20):
    return pltpu.CompilerParams(vmem_limit_bytes=limit * 1024 * 1024)


def cost(flops, moved):
    return pl.CostEstimate(flops=flops // 1000, bytes_accessed=moved // 1000, transcendentals=0)


def diagonal_mask(rows, width):
    row = lax.broadcasted_iota(I32, (rows, width), 0)
    lane = lax.broadcasted_iota(I32, (rows, width), 1)
    return row == lane


def encode(value, out_ref, start=0):
    rows, width = value.shape
    largest = jnp.maximum(jnp.max(jnp.abs(value), axis=1, keepdims=True), 1e-30)
    level = jnp.ceil(jnp.log(largest * (1.0 / TOP)) * (STEPS / LN2))
    coded = jnp.round(value * jnp.exp2(level * (-1.0 / STEPS)))
    out_ref[start : start + rows, :] = coded.astype(I32).astype(I16)
    line = jnp.sum(jnp.where(diagonal_mask(rows, width), level, 0.0), axis=0, keepdims=True)
    lines = jnp.broadcast_to(line, (EXTRA, width))
    out_ref[start + rows : start + rows + EXTRA, :] = lines.astype(I32).astype(I16)


def decode(in_ref, start=0, rows=None):
    rows, width = rows or in_ref.shape[0] - EXTRA, in_ref.shape[1]
    coded = in_ref[start : start + rows, :].astype(I32).astype(F32)
    line = in_ref[start + rows : start + rows + EXTRA, :].astype(I32).astype(F32)[:1]
    level = jnp.sum(
        jnp.where(diagonal_mask(rows, width), jnp.broadcast_to(line, (rows, width)), 0.0),
        axis=1,
        keepdims=True,
    )
    return coded * jnp.exp2(level * (1.0 / STEPS))


def product_kernel(panels, at_ref, a_ref, own_ref, other_ref, *refs):
    outs, m_ref = refs[: 4 * panels], refs[4 * panels]
    step = pl.program_id(0)
    shard = own_ref.shape[3]

    @pl.when(step == 0)
    def _():
        core, h, t = at_ref[1], at_ref[2], at_ref[3]
        for p in range(panels):
            for k in range(4):
                for i in range(2):
                    base = (k ^ t) * (4 * shard) + (i ^ h) * shard
                    first = pl.multiple_of(base + core * (2 * shard), 32)
                    second = pl.multiple_of(base + (1 - core) * (2 * shard), 32)
                    m_ref[p, pl.ds(first, shard), :] = own_ref[k, i, p]
                    m_ref[p, pl.ds(second, shard), :] = other_ref[k, i, p]

    block = a_ref[...]
    lines = block.reshape(4 * block.shape[2], block.shape[3])
    for p in range(panels):
        value = jnp.dot(lines, m_ref[p], preferred_element_type=F32)
        for at in range(3):

            @pl.when(step == at)
            def _(ref=outs[4 * p + 1 + at], value=value):
                encode(value, ref)

        @pl.when(step == 3)
        def _(ref=outs[4 * p], value=value):
            ref[...] = value


def product(at, a4, own, other, first=0):
    shard, order = a4.shape[2], a4.shape[3]
    panels, width = 1, own.shape[4]
    rows = 4 * shard
    whole = pl.BlockSpec((4, 2, panels, shard, width), lambda g, s: (0, 0, first, 0, 0))
    kept = pl.BlockSpec((rows, width), lambda g, s: (0, 0))
    coded = pl.BlockSpec((rows + EXTRA, width), lambda g, s: (0, 0))
    one = [jax.ShapeDtypeStruct((rows, width), F32)]
    one += [jax.ShapeDtypeStruct((rows + EXTRA, width), I16)] * 3
    outs = pl.pallas_call(
        functools.partial(product_kernel, panels),
        grid_spec=pltpu.PrefetchScalarGridSpec(
            num_scalar_prefetch=1,
            grid=(4,),
            in_specs=[
                pl.BlockSpec(
                    (4, 1, shard, order), lambda g, s: (0, s[0] ^ ((g + 1) & 3), 0, 0)
                ),
                whole,
                whole,
            ],
            out_specs=([kept] + [coded] * 3) * panels,
            scratch_shapes=[pltpu.VMEM((panels, order, width), BF16)],
        ),
        out_shape=one * panels,
        compiler_params=params(44),
        cost_estimate=cost(8 * panels * rows * order * width, 2 * order * order),
        name="product",
    )(at, a4, own, other)
    return [outs[4 * p : 4 * p + 4] for p in range(panels)]


def middle_kernel(panels, base, *refs):
    at_ref, refs = refs[0], refs[1:]
    keeps, refs = refs[:panels], refs[panels:]
    parts, refs = refs[: 3 * panels], refs[3 * panels :]
    masked, refs = refs[:4], refs[4:]
    own_ref, *coded = refs[:4]
    mine_ref, theirs_ref, sum_ref, m_ref = refs[4:]
    shard = own_ref.shape[0] // panels
    half = mine_ref.shape[0] // panels
    core, l = at_ref[1], at_ref[4]

    def place(k):
        return pl.ds(pl.multiple_of((l ^ k) * shard, 32), shard)

    for p in range(panels):
        value = keeps[p][...]
        for ref in parts[3 * p : 3 * p + 3]:
            value = value + decode(ref)
        sum_ref[...] = value
        own_ref[p * shard : (p + 1) * shard, :] = sum_ref[place(0), :]
        for k in (1, 2, 3):
            encode(sum_ref[place(k), :], coded[k - 1], p * (shard + EXTRA))
        for k, ref in enumerate(masked):
            m_ref[place(k), :] = ref[base + p]
        high = value.astype(BF16)
        rest = value - high.astype(F32)
        mid = rest.astype(BF16)
        low = (rest - mid.astype(F32)).astype(BF16)
        for which, out in ((core, mine_ref), (1 - core, theirs_ref)):
            left = m_ref[:, pl.ds(pl.multiple_of(which * half, 128), half)]
            dims = (((0,), (0,)), ((), ()))
            terms = [
                lax.dot_general(left, r, dims, preferred_element_type=F32) for r in (low, mid, high)
            ]
            out[p * half : (p + 1) * half, :] = (terms[0] + terms[1]) + terms[2]


def middle(at, keeps, parts, masked, base):
    rows, width = keeps[0].shape
    panels, shard = len(keeps), rows // 4
    return pl.pallas_call(
        functools.partial(middle_kernel, panels, base),
        in_specs=[SMEM] + [VMEM] * (4 * panels + 4),
        out_specs=[VMEM] * 6,
        out_shape=[jax.ShapeDtypeStruct((panels * shard, width), F32)]
        + [jax.ShapeDtypeStruct((panels * (shard + EXTRA), width), I16)] * 3
        + [jax.ShapeDtypeStruct((panels * (width // 2), width), F32)] * 2,
        scratch_shapes=[pltpu.VMEM((rows, width), F32), pltpu.VMEM((rows, width), BF16)],
        compiler_params=params(),
        cost_estimate=cost(6 * rows * width * width, 16 * rows * width),
        name="middle",
    )(at, *keeps, *sum(parts, []), *masked)


def last_kernel(groups, *refs):
    out_ref = refs[-1]
    shard = out_ref.shape[1]
    for g, which in enumerate(groups):
        own_ref, *parts = refs[4 * g : 4 * g + 4]
        for p, panel in enumerate(which):
            total = own_ref[p * shard : (p + 1) * shard, :]
            for ref in parts:
                total = total + decode(ref, p * (shard + EXTRA), shard)
            out_ref[panel] = -total


def last(groups, shape):
    ins = [ref for own, parts, _ in groups for ref in (own, *parts)]
    return pl.pallas_call(
        functools.partial(last_kernel, [which for _, _, which in groups]),
        in_specs=[VMEM] * len(ins),
        out_specs=VMEM,
        out_shape=jax.ShapeDtypeStruct(shape, F32),
        compiler_params=params(),
        cost_estimate=cost(8 * shape[1] * shape[2], 16 * shape[1] * shape[2]),
        name="last",
    )(*ins)


def encode_lanes(value, out_ref, start=0):
    rows, width = value.shape
    largest = jnp.maximum(jnp.max(jnp.abs(value), axis=1, keepdims=True), 1e-30)
    level = jnp.ceil(jnp.log(largest * (1.0 / TOP)) * (STEPS / LN2))
    coded = jnp.round(value * jnp.exp2(level * (-1.0 / STEPS)))
    out_ref[start : start + rows, :width] = coded.astype(I32).astype(I16)
    lanes = jnp.broadcast_to(level, (rows, LANES))
    out_ref[start : start + rows, width:] = lanes.astype(I32).astype(I16)


def decode_lanes(block):
    width = block.shape[1] - LANES
    coded = block[:, :width].astype(I32).astype(F32)
    level = block[:, width:].astype(I32).astype(F32)[:, :1]
    return coded * jnp.exp2(level * (1.0 / STEPS))


def fold_kernel(*refs):
    out, count = refs[-1], len(refs) // 2
    start = 0
    for p in range(count):
        rows = refs[p].shape[0]
        encode_lanes(refs[p][...] + refs[count + p][...], out, start)
        start += rows


def fold(mines, theirs):
    width = mines[0].shape[1]
    total = sum(mine.shape[0] for mine in mines)
    return pl.pallas_call(
        fold_kernel,
        in_specs=[VMEM] * (2 * len(mines)),
        out_specs=VMEM,
        out_shape=jax.ShapeDtypeStruct((total, width + LANES), I16),
        compiler_params=params(),
        cost_estimate=cost(total * width, 12 * total * width),
        name="fold",
    )(*mines, *theirs)


def gathered_kernel(in_ref, out_ref):
    total = decode_lanes(in_ref[0])
    for k in range(1, in_ref.shape[0]):
        total = total + decode_lanes(in_ref[k])
    out_ref[...] = total


def gathered(pieces):
    count, rows, lanes = pieces.shape
    return pl.pallas_call(
        gathered_kernel,
        in_specs=[VMEM],
        out_specs=VMEM,
        out_shape=jax.ShapeDtypeStruct((rows, lanes - LANES), F32),
        compiler_params=params(),
        cost_estimate=cost(count * rows * lanes, 2 * count * rows * lanes),
        name="gathered",
    )(pieces)


def copies_kernel(own_ref, r1_ref, r2_ref, r3_ref, out_ref):
    total = (own_ref[...] + r1_ref[...]) + (r2_ref[...] + r3_ref[...])
    encode_lanes(total, out_ref.at[0])
    for k in range(1, out_ref.shape[0]):
        out_ref[k] = out_ref[0]


def copies(own, found):
    rows, width = own.shape
    return pl.pallas_call(
        copies_kernel,
        in_specs=[VMEM] * 4,
        out_specs=VMEM,
        out_shape=jax.ShapeDtypeStruct((16, rows, width + LANES), I16),
        compiler_params=params(),
        cost_estimate=cost(rows * width, 32 * rows * width),
        name="copies",
    )(own, *found)


def finish_kernel(at_ref, mine_ref, theirs_ref, diag_ref, out_ref):
    half = diag_ref.shape[1] // 2
    core = at_ref[1]
    for p in range(diag_ref.shape[0]):
        for which, ref in ((core, mine_ref), (1 - core, theirs_ref)):
            place = pl.ds(pl.multiple_of(which * half, 8), half)
            part = decode_lanes(ref[p * half : (p + 1) * half, :])
            out_ref[p, place, :] = diag_ref[p, place, :] + part


def finish(at, mine, theirs, diag):
    return pl.pallas_call(
        finish_kernel,
        in_specs=[SMEM] + [VMEM] * 3,
        out_specs=VMEM,
        out_shape=jax.ShapeDtypeStruct(diag.shape, F32),
        compiler_params=params(),
        cost_estimate=cost(diag.size, 12 * diag.size),
        name="finish",
    )(at, mine, theirs, diag)


def after(values, *earlier):
    return lax.optimization_barrier((values, earlier))[0]


def body(ancestor_inverse, panels, diag_inverse, tile_mask):
    x, h, core, l, y = (lax.axis_index(axis) for axis in AXES)
    at = jnp.stack([y, core, h, x ^ l, l, x]).astype(I32)
    kept, count, width = panels.shape
    order = ancestor_inverse.shape[1]
    tiles = tile_mask.shape[1]
    start = (((x * 2 + h) * 2 + core) * 16 + l * 4 + y) * kept
    tile = start // TILE
    first = lax.dynamic_slice_in_dim(tile_mask, tile, 1, 1)
    second = lax.dynamic_slice_in_dim(tile_mask, jnp.minimum(tile + 1, tiles - 1), 1, 1)
    in_first = start + jnp.arange(kept) < (tile + 1) * TILE
    own_mask = jnp.where(in_first[None, :], first, second).astype(BF16)
    masked = jnp.swapaxes(panels, 0, 1) * own_mask[:, :, None]

    def gather(message):
        return [message] + [send(message, over_x(k)) for k in (1, 2, 3)]

    a4 = ancestor_inverse.reshape(4, 4, kept, order)
    moved_a, moved_b = send(masked[2:], spread), send(masked[:2], spread)
    turned_a = [send(moved_a, turn(i)) for i in range(2)]
    turned_b = [send(moved_b, turn(i)) for i in range(2)]
    own_a = gather(after(jnp.stack(turned_a), moved_b))
    own_a = after(jnp.stack(own_a), turned_b)
    own_b = gather(after(jnp.stack(turned_b), own_a))
    ((keep_a, *coded),) = product(at, a4, own_a, send(own_a, over_core))
    parts_a = [send(coded[k - 1], over_y(k)) for k in (1, 2, 3)]
    own_b = after(jnp.stack(own_b), parts_a[0], parts_a[2])
    other_b = send(own_b, over_core)
    ((keep_b, *coded),) = product(at, a4, own_b, other_b)
    parts_b = [send(q, over_y(k)) for k, q in zip((1, 2, 3), after(coded, parts_a[0], parts_a[2]))]
    ((keep_c, *coded),) = product(at, a4, own_b, other_b, 1)
    parts_c = [send(q, over_y(k)) for k, q in zip((1, 2, 3), coded)]
    late = after(masked, keep_c)
    beside = [masked] + [send(late, over_l(k)) for k in (1, 2, 3)]
    parts_b = after(parts_b, keep_c)
    own_2, *coded = middle(at, [keep_a], [after(parts_a, parts_b)], beside, 2)
    coded_2, (mine_2, their_2) = coded[:3], coded[3:]
    swapped_2 = send(their_2, over_core)
    found_2 = [send(coded_2[k - 1], over_l(k)) for k in (1, 2, 3)]
    parts_c = after(parts_c, mine_2)
    own_01, *coded = middle(at, [keep_b, keep_c], [parts_b, parts_c], beside, 0)
    coded_01, (mine_01, their_01) = coded[:3], coded[3:]
    swapped_01 = send(their_01, over_core)
    halves = fold([mine_01, after(mine_2, found_2)], [swapped_01, swapped_2])
    found_01 = [send(coded_01[k - 1], over_l(k)) for k in (1, 2, 3)]
    pieces = halves.reshape(16, -1, width + LANES)
    total = gathered(lax.all_to_all(pieces, ("x", "y"), 0, 0))
    found_01 = after(found_01, total)
    total = total + send(total, over_h)
    beyond = [send(total, over_l(k)) for k in (1, 2, 3)]
    pieces = copies(total, after(beyond, found_01))
    mine = lax.all_to_all(pieces, ("x", "y"), 0, 0).reshape(halves.shape)
    blocks = last([(own_01, found_01, (0, 1)), (own_2, found_2, (2,))], masked.shape)
    diagonal = finish(at, mine, send(mine, over_core), diag_inverse)
    return jnp.swapaxes(blocks, 0, 1), diagonal


def solution(mesh):
    finer = Mesh(mesh.devices.reshape(SIZES), AXES)
    placed = (P(ROW, COL), P(AXES, None, None), P(), P())
    return jax.shard_map(
        body, mesh=finer, in_specs=placed, out_specs=(P(AXES, None, None), P()), check_vma=False
    )
```

```python
import functools

import jax
import jax.numpy as jnp
from jax import lax
from jax.experimental import pallas as pl
from jax.experimental.pallas import tpu as pltpu
from jax.sharding import Mesh
from jax.sharding import PartitionSpec as P

TILE = 128
AXES = ("x", "h", "core", "l", "y")
SIZES = (4, 2, 2, 4, 4)
ROW = ("x", "h", "core")
COL = ("l", "y")
EXTRA = 16
LANES = 128
STEPS = 64.0
TOP = 32766.0
LN2 = 0.6931471805599453
VMEM = pl.BlockSpec(memory_space=pltpu.VMEM)
SMEM = pl.BlockSpec(memory_space=pltpu.SMEM)
F32, BF16, I16, I32 = jnp.float32, jnp.bfloat16, jnp.int16, jnp.int32


def coords(device):
    out = []
    for size in SIZES[::-1]:
        out.append(device % size)
        device //= size
    return tuple(out[::-1])


def number(place):
    value = 0
    for size, at in zip(SIZES, place):
        value = value * size + at
    return value


def send(value, move):
    pairs = [(d, number(move(*coords(d)))) for d in range(256)]
    return lax.ppermute(value, AXES, pairs)


def over_x(k):
    return lambda x, h, c, l, y: (x ^ k, h, c, l, y)


def over_y(k):
    return lambda x, h, c, l, y: (x, h, c, l, y ^ k)


def over_l(k):
    return lambda x, h, c, l, y: (x, h, c, l ^ k, y)


def over_h(x, h, c, l, y):
    return (x, 1 - h, c, l, y)


def over_core(x, h, c, l, y):
    return (x, h, 1 - c, l, y)


def spread(x, h, c, l, y):
    return (x ^ l, h, c, l, y)


def turn(i):
    return lambda x, h, c, l, y: (x, (y & 1) ^ i, y >> 1, x ^ l, 2 * h + c)


def params(limit=20):
    return pltpu.CompilerParams(vmem_limit_bytes=limit * 1024 * 1024)


def cost(flops, moved):
    return pl.CostEstimate(flops=flops // 1000, bytes_accessed=moved // 1000, transcendentals=0)


def diagonal_mask(rows, width):
    row = lax.broadcasted_iota(I32, (rows, width), 0)
    lane = lax.broadcasted_iota(I32, (rows, width), 1)
    return row == lane


def encode(value, out_ref, start=0):
    rows, width = value.shape
    largest = jnp.maximum(jnp.max(jnp.abs(value), axis=1, keepdims=True), 1e-30)
    level = jnp.ceil(jnp.log(largest * (1.0 / TOP)) * (STEPS / LN2))
    coded = jnp.round(value * jnp.exp2(level * (-1.0 / STEPS)))
    out_ref[start : start + rows, :] = coded.astype(I32).astype(I16)
    line = jnp.sum(jnp.where(diagonal_mask(rows, width), level, 0.0), axis=0, keepdims=True)
    lines = jnp.broadcast_to(line, (EXTRA, width))
    out_ref[start + rows : start + rows + EXTRA, :] = lines.astype(I32).astype(I16)


def decode(in_ref, start=0, rows=None):
    rows, width = rows or in_ref.shape[0] - EXTRA, in_ref.shape[1]
    coded = in_ref[start : start + rows, :].astype(I32).astype(F32)
    line = in_ref[start + rows : start + rows + EXTRA, :].astype(I32).astype(F32)[:1]
    level = jnp.sum(
        jnp.where(diagonal_mask(rows, width), jnp.broadcast_to(line, (rows, width)), 0.0),
        axis=1,
        keepdims=True,
    )
    return coded * jnp.exp2(level * (1.0 / STEPS))


def product_kernel(panels, at_ref, a_ref, own_ref, other_ref, *refs):
    outs, m_ref = refs[: 4 * panels], refs[4 * panels]
    step = pl.program_id(0)
    shard = own_ref.shape[3]

    @pl.when(step == 0)
    def _():
        core, h, t = at_ref[1], at_ref[2], at_ref[3]
        for p in range(panels):
            for k in range(4):
                for i in range(2):
                    base = (k ^ t) * (4 * shard) + (i ^ h) * shard
                    first = pl.multiple_of(base + core * (2 * shard), 32)
                    second = pl.multiple_of(base + (1 - core) * (2 * shard), 32)
                    m_ref[p, pl.ds(first, shard), :] = own_ref[k, i, p]
                    m_ref[p, pl.ds(second, shard), :] = other_ref[k, i, p]

    block = a_ref[...]
    lines = block.reshape(4 * block.shape[2], block.shape[3])
    for p in range(panels):
        value = jnp.dot(lines, m_ref[p], preferred_element_type=F32)
        for at in range(3):

            @pl.when(step == at)
            def _(ref=outs[4 * p + 1 + at], value=value):
                encode(value, ref)

        @pl.when(step == 3)
        def _(ref=outs[4 * p], value=value):
            ref[...] = value


def product(at, a4, own, other, first=0):
    shard, order = a4.shape[2], a4.shape[3]
    panels, width = 1, own.shape[4]
    rows = 4 * shard
    whole = pl.BlockSpec((4, 2, panels, shard, width), lambda g, s: (0, 0, first, 0, 0))
    kept = pl.BlockSpec((rows, width), lambda g, s: (0, 0))
    coded = pl.BlockSpec((rows + EXTRA, width), lambda g, s: (0, 0))
    one = [jax.ShapeDtypeStruct((rows, width), F32)]
    one += [jax.ShapeDtypeStruct((rows + EXTRA, width), I16)] * 3
    outs = pl.pallas_call(
        functools.partial(product_kernel, panels),
        grid_spec=pltpu.PrefetchScalarGridSpec(
            num_scalar_prefetch=1,
            grid=(4,),
            in_specs=[
                pl.BlockSpec(
                    (4, 1, shard, order), lambda g, s: (0, s[0] ^ ((g + 1) & 3), 0, 0)
                ),
                whole,
                whole,
            ],
            out_specs=([kept] + [coded] * 3) * panels,
            scratch_shapes=[pltpu.VMEM((panels, order, width), BF16)],
        ),
        out_shape=one * panels,
        compiler_params=params(44),
        cost_estimate=cost(8 * panels * rows * order * width, 2 * order * order),
        name="product",
    )(at, a4, own, other)
    return [outs[4 * p : 4 * p + 4] for p in range(panels)]


def middle_kernel(panels, base, *refs):
    at_ref, refs = refs[0], refs[1:]
    keeps, refs = refs[:panels], refs[panels:]
    parts, refs = refs[: 3 * panels], refs[3 * panels :]
    masked, refs = refs[:4], refs[4:]
    own_ref, *coded = refs[:4]
    mine_ref, theirs_ref, sum_ref, m_ref = refs[4:]
    shard = own_ref.shape[0] // panels
    half = mine_ref.shape[0] // panels
    core, l = at_ref[1], at_ref[4]

    def place(k):
        return pl.ds(pl.multiple_of((l ^ k) * shard, 32), shard)

    for p in range(panels):
        value = keeps[p][...]
        for ref in parts[3 * p : 3 * p + 3]:
            value = value + decode(ref)
        sum_ref[...] = value
        own_ref[p * shard : (p + 1) * shard, :] = sum_ref[place(0), :]
        for k in (1, 2, 3):
            encode(sum_ref[place(k), :], coded[k - 1], p * (shard + EXTRA))
        for k, ref in enumerate(masked):
            m_ref[place(k), :] = ref[base + p]
        high = value.astype(BF16)
        rest = value - high.astype(F32)
        mid = rest.astype(BF16)
        low = (rest - mid.astype(F32)).astype(BF16)
        for which, out in ((core, mine_ref), (1 - core, theirs_ref)):
            left = m_ref[:, pl.ds(pl.multiple_of(which * half, 128), half)]
            dims = (((0,), (0,)), ((), ()))
            terms = [
                lax.dot_general(left, r, dims, preferred_element_type=F32) for r in (low, mid, high)
            ]
            out[p * half : (p + 1) * half, :] = (terms[0] + terms[1]) + terms[2]


def middle(at, keeps, parts, masked, base):
    rows, width = keeps[0].shape
    panels, shard = len(keeps), rows // 4
    return pl.pallas_call(
        functools.partial(middle_kernel, panels, base),
        in_specs=[SMEM] + [VMEM] * (4 * panels + 4),
        out_specs=[VMEM] * 6,
        out_shape=[jax.ShapeDtypeStruct((panels * shard, width), F32)]
        + [jax.ShapeDtypeStruct((panels * (shard + EXTRA), width), I16)] * 3
        + [jax.ShapeDtypeStruct((panels * (width // 2), width), F32)] * 2,
        scratch_shapes=[pltpu.VMEM((rows, width), F32), pltpu.VMEM((rows, width), BF16)],
        compiler_params=params(),
        cost_estimate=cost(6 * rows * width * width, 16 * rows * width),
        name="middle",
    )(at, *keeps, *sum(parts, []), *masked)


def last_kernel(groups, *refs):
    out_ref = refs[-1]
    shard = out_ref.shape[1]
    for g, which in enumerate(groups):
        own_ref, *parts = refs[4 * g : 4 * g + 4]
        for p, panel in enumerate(which):
            total = own_ref[p * shard : (p + 1) * shard, :]
            for ref in parts:
                total = total + decode(ref, p * (shard + EXTRA), shard)
            out_ref[panel] = -total


def last(groups, shape):
    ins = [ref for own, parts, _ in groups for ref in (own, *parts)]
    return pl.pallas_call(
        functools.partial(last_kernel, [which for _, _, which in groups]),
        in_specs=[VMEM] * len(ins),
        out_specs=VMEM,
        out_shape=jax.ShapeDtypeStruct(shape, F32),
        compiler_params=params(),
        cost_estimate=cost(8 * shape[1] * shape[2], 16 * shape[1] * shape[2]),
        name="last",
    )(*ins)


def encode_lanes(value, out_ref, start=0):
    rows, width = value.shape
    largest = jnp.maximum(jnp.max(jnp.abs(value), axis=1, keepdims=True), 1e-30)
    level = jnp.ceil(jnp.log(largest * (1.0 / TOP)) * (STEPS / LN2))
    coded = jnp.round(value * jnp.exp2(level * (-1.0 / STEPS)))
    out_ref[start : start + rows, :width] = coded.astype(I32).astype(I16)
    lanes = jnp.broadcast_to(level, (rows, LANES))
    out_ref[start : start + rows, width:] = lanes.astype(I32).astype(I16)


def decode_lanes(block):
    width = block.shape[1] - LANES
    coded = block[:, :width].astype(I32).astype(F32)
    level = block[:, width:].astype(I32).astype(F32)[:, :1]
    return coded * jnp.exp2(level * (1.0 / STEPS))


def fold_kernel(*refs):
    out, count = refs[-1], len(refs) // 2
    start = 0
    for p in range(count):
        rows = refs[p].shape[0]
        encode_lanes(refs[p][...] + refs[count + p][...], out, start)
        start += rows


def fold(mines, theirs):
    width = mines[0].shape[1]
    total = sum(mine.shape[0] for mine in mines)
    return pl.pallas_call(
        fold_kernel,
        in_specs=[VMEM] * (2 * len(mines)),
        out_specs=VMEM,
        out_shape=jax.ShapeDtypeStruct((total, width + LANES), I16),
        compiler_params=params(),
        cost_estimate=cost(total * width, 12 * total * width),
        name="fold",
    )(*mines, *theirs)


def gathered_kernel(in_ref, out_ref):
    total = decode_lanes(in_ref[0])
    for k in range(1, in_ref.shape[0]):
        total = total + decode_lanes(in_ref[k])
    out_ref[...] = total


def gathered(pieces):
    count, rows, lanes = pieces.shape
    return pl.pallas_call(
        gathered_kernel,
        in_specs=[VMEM],
        out_specs=VMEM,
        out_shape=jax.ShapeDtypeStruct((rows, lanes - LANES), F32),
        compiler_params=params(),
        cost_estimate=cost(count * rows * lanes, 2 * count * rows * lanes),
        name="gathered",
    )(pieces)


def copies_kernel(own_ref, r1_ref, r2_ref, r3_ref, out_ref):
    total = (own_ref[...] + r1_ref[...]) + (r2_ref[...] + r3_ref[...])
    encode_lanes(total, out_ref.at[0])
    for k in range(1, out_ref.shape[0]):
        out_ref[k] = out_ref[0]


def copies(own, found):
    rows, width = own.shape
    return pl.pallas_call(
        copies_kernel,
        in_specs=[VMEM] * 4,
        out_specs=VMEM,
        out_shape=jax.ShapeDtypeStruct((16, rows, width + LANES), I16),
        compiler_params=params(),
        cost_estimate=cost(rows * width, 32 * rows * width),
        name="copies",
    )(own, *found)


def finish_kernel(at_ref, mine_ref, theirs_ref, diag_ref, out_ref):
    half = diag_ref.shape[1] // 2
    core = at_ref[1]
    for p in range(diag_ref.shape[0]):
        for which, ref in ((core, mine_ref), (1 - core, theirs_ref)):
            place = pl.ds(pl.multiple_of(which * half, 8), half)
            part = decode_lanes(ref[p * half : (p + 1) * half, :])
            out_ref[p, place, :] = diag_ref[p, place, :] + part


def finish(at, mine, theirs, diag):
    return pl.pallas_call(
        finish_kernel,
        in_specs=[SMEM] + [VMEM] * 3,
        out_specs=VMEM,
        out_shape=jax.ShapeDtypeStruct(diag.shape, F32),
        compiler_params=params(),
        cost_estimate=cost(diag.size, 12 * diag.size),
        name="finish",
    )(at, mine, theirs, diag)


def after(values, *earlier):
    return lax.optimization_barrier((values, earlier))[0]


def body(ancestor_inverse, panels, diag_inverse, tile_mask):
    x, h, core, l, y = (lax.axis_index(axis) for axis in AXES)
    at = jnp.stack([y, core, h, x ^ l, l, x]).astype(I32)
    kept, count, width = panels.shape
    order = ancestor_inverse.shape[1]
    tiles = tile_mask.shape[1]
    start = (((x * 2 + h) * 2 + core) * 16 + l * 4 + y) * kept
    tile = start // TILE
    first = lax.dynamic_slice_in_dim(tile_mask, tile, 1, 1)
    second = lax.dynamic_slice_in_dim(tile_mask, jnp.minimum(tile + 1, tiles - 1), 1, 1)
    in_first = start + jnp.arange(kept) < (tile + 1) * TILE
    own_mask = jnp.where(in_first[None, :], first, second).astype(BF16)
    masked = jnp.swapaxes(panels, 0, 1) * own_mask[:, :, None]

    def gather(message):
        return [message] + [send(message, over_x(k)) for k in (1, 2, 3)]

    a4 = ancestor_inverse.reshape(4, 4, kept, order)
    moved_a, moved_b = send(masked[2:], spread), send(masked[:2], spread)
    turned_a = [send(moved_a, turn(i)) for i in range(2)]
    turned_b = [send(moved_b, turn(i)) for i in range(2)]
    own_a = gather(after(jnp.stack(turned_a), moved_b))
    own_a = after(jnp.stack(own_a), turned_b)
    own_b = gather(after(jnp.stack(turned_b), own_a))
    ((keep_a, *coded),) = product(at, a4, own_a, send(own_a, over_core))
    parts_a = [send(coded[k - 1], over_y(k)) for k in (1, 2, 3)]
    far = send(after(masked, own_a), over_l(2))
    own_b = after(jnp.stack(own_b), parts_a[0], parts_a[2])
    other_b = send(own_b, over_core)
    ((keep_b, *coded),) = product(at, a4, own_b, other_b)
    parts_b = [send(q, over_y(k)) for k, q in zip((1, 2, 3), after(coded, parts_a[0], parts_a[2]))]
    ((keep_c, *coded),) = product(after(at, far), a4, own_b, other_b, 1)
    parts_c = [send(q, over_y(k)) for k, q in zip((1, 2, 3), coded)]
    late = after(masked, keep_c)
    beside = [masked, send(late, over_l(1)), far, send(late, over_l(3))]
    parts_b = after(parts_b, keep_c)
    own_2, *coded = middle(at, [keep_a], [after(parts_a, parts_b)], beside, 2)
    coded_2, (mine_2, their_2) = coded[:3], coded[3:]
    swapped_2 = send(their_2, over_core)
    found_2 = [send(coded_2[k - 1], over_l(k)) for k in (1, 2, 3)]
    parts_c = after(parts_c, mine_2)
    own_01, *coded = middle(at, [keep_b, keep_c], [parts_b, parts_c], beside, 0)
    coded_01, (mine_01, their_01) = coded[:3], coded[3:]
    swapped_01 = send(their_01, over_core)
    halves = fold([mine_01, mine_2], [swapped_01, swapped_2])
    found_01 = [send(coded_01[k - 1], over_l(k)) for k in (1, 2, 3)]
    pieces = halves.reshape(16, -1, width + LANES)
    total = gathered(lax.all_to_all(pieces, ("x", "y"), 0, 0))
    found_01 = after(found_01, total)
    total = total + send(total, over_h)
    beyond = [send(total, over_l(k)) for k in (1, 2, 3)]
    pieces = copies(total, after(beyond, found_01))
    mine = after(lax.all_to_all(pieces, ("x", "y"), 0, 0), found_2).reshape(halves.shape)
    blocks = last([(own_01, found_01, (0, 1)), (own_2, found_2, (2,))], masked.shape)
    diagonal = finish(at, mine, send(mine, over_core), diag_inverse)
    return jnp.swapaxes(blocks, 0, 1), diagonal


def solution(mesh):
    finer = Mesh(mesh.devices.reshape(SIZES), AXES)
    placed = (P(ROW, COL), P(AXES, None, None), P(), P())
    return jax.shard_map(
        body, mesh=finer, in_specs=placed, out_specs=(P(AXES, None, None), P()), check_vma=False
    )
```

```python
import functools

import jax
import jax.numpy as jnp
from jax import lax
from jax.experimental import pallas as pl
from jax.experimental.pallas import tpu as pltpu
from jax.sharding import Mesh
from jax.sharding import PartitionSpec as P

TILE = 128
AXES = ("x", "h", "core", "l", "y")
SIZES = (4, 2, 2, 4, 4)
ROW = ("x", "h", "core")
COL = ("l", "y")
EXTRA = 16
LANES = 128
STEPS = 64.0
TOP = 32766.0
LN2 = 0.6931471805599453
VMEM = pl.BlockSpec(memory_space=pltpu.VMEM)
SMEM = pl.BlockSpec(memory_space=pltpu.SMEM)
F32, BF16, I16, I32 = jnp.float32, jnp.bfloat16, jnp.int16, jnp.int32


def coords(device):
    out = []
    for size in SIZES[::-1]:
        out.append(device % size)
        device //= size
    return tuple(out[::-1])


def number(place):
    value = 0
    for size, at in zip(SIZES, place):
        value = value * size + at
    return value


def send(value, move):
    pairs = [(d, number(move(*coords(d)))) for d in range(256)]
    return lax.ppermute(value, AXES, pairs)


def over_x(k):
    return lambda x, h, c, l, y: (x ^ k, h, c, l, y)


def over_y(k):
    return lambda x, h, c, l, y: (x, h, c, l, y ^ k)


def over_l(k):
    return lambda x, h, c, l, y: (x, h, c, l ^ k, y)


def over_h(x, h, c, l, y):
    return (x, 1 - h, c, l, y)


def over_core(x, h, c, l, y):
    return (x, h, 1 - c, l, y)


def spread(x, h, c, l, y):
    return (x ^ l, h, c, l, y)


def turn(i):
    return lambda x, h, c, l, y: (x, (y & 1) ^ i, y >> 1, x ^ l, 2 * h + c)


def params(limit=20):
    return pltpu.CompilerParams(vmem_limit_bytes=limit * 1024 * 1024)


def cost(flops, moved):
    return pl.CostEstimate(flops=flops // 1000, bytes_accessed=moved // 1000, transcendentals=0)


def diagonal_mask(rows, width):
    row = lax.broadcasted_iota(I32, (rows, width), 0)
    lane = lax.broadcasted_iota(I32, (rows, width), 1)
    return row == lane


def encode(value, out_ref, start=0):
    rows, width = value.shape
    largest = jnp.maximum(jnp.max(jnp.abs(value), axis=1, keepdims=True), 1e-30)
    level = jnp.ceil(jnp.log(largest * (1.0 / TOP)) * (STEPS / LN2))
    coded = jnp.round(value * jnp.exp2(level * (-1.0 / STEPS)))
    out_ref[start : start + rows, :] = coded.astype(I32).astype(I16)
    line = jnp.sum(jnp.where(diagonal_mask(rows, width), level, 0.0), axis=0, keepdims=True)
    lines = jnp.broadcast_to(line, (EXTRA, width))
    out_ref[start + rows : start + rows + EXTRA, :] = lines.astype(I32).astype(I16)


def decode(in_ref, start=0, rows=None):
    rows, width = rows or in_ref.shape[0] - EXTRA, in_ref.shape[1]
    coded = in_ref[start : start + rows, :].astype(I32).astype(F32)
    line = in_ref[start + rows : start + rows + EXTRA, :].astype(I32).astype(F32)[:1]
    level = jnp.sum(
        jnp.where(diagonal_mask(rows, width), jnp.broadcast_to(line, (rows, width)), 0.0),
        axis=1,
        keepdims=True,
    )
    return coded * jnp.exp2(level * (1.0 / STEPS))


def product_kernel(panels, at_ref, a_ref, own_ref, other_ref, *refs):
    outs, m_ref = refs[: 4 * panels], refs[4 * panels]
    step = pl.program_id(0)
    shard = own_ref.shape[3]

    @pl.when(step == 0)
    def _():
        core, h, t = at_ref[1], at_ref[2], at_ref[3]
        for p in range(panels):
            for k in range(4):
                for i in range(2):
                    base = (k ^ t) * (4 * shard) + (i ^ h) * shard
                    first = pl.multiple_of(base + core * (2 * shard), 32)
                    second = pl.multiple_of(base + (1 - core) * (2 * shard), 32)
                    m_ref[p, pl.ds(first, shard), :] = own_ref[k, i, p]
                    m_ref[p, pl.ds(second, shard), :] = other_ref[k, i, p]

    block = a_ref[...]
    lines = block.reshape(4 * block.shape[2], block.shape[3])
    for p in range(panels):
        value = jnp.dot(lines, m_ref[p], preferred_element_type=F32)
        for at in range(3):

            @pl.when(step == at)
            def _(ref=outs[4 * p + 1 + at], value=value):
                encode(value, ref)

        @pl.when(step == 3)
        def _(ref=outs[4 * p], value=value):
            ref[...] = value


def product(at, a4, own, other, first=0):
    shard, order = a4.shape[2], a4.shape[3]
    panels, width = 1, own.shape[4]
    rows = 4 * shard
    whole = pl.BlockSpec((4, 2, panels, shard, width), lambda g, s: (0, 0, first, 0, 0))
    kept = pl.BlockSpec((rows, width), lambda g, s: (0, 0))
    coded = pl.BlockSpec((rows + EXTRA, width), lambda g, s: (0, 0))
    one = [jax.ShapeDtypeStruct((rows, width), F32)]
    one += [jax.ShapeDtypeStruct((rows + EXTRA, width), I16)] * 3
    outs = pl.pallas_call(
        functools.partial(product_kernel, panels),
        grid_spec=pltpu.PrefetchScalarGridSpec(
            num_scalar_prefetch=1,
            grid=(4,),
            in_specs=[
                pl.BlockSpec(
                    (4, 1, shard, order), lambda g, s: (0, s[0] ^ ((g + 1) & 3), 0, 0)
                ),
                whole,
                whole,
            ],
            out_specs=([kept] + [coded] * 3) * panels,
            scratch_shapes=[pltpu.VMEM((panels, order, width), BF16)],
        ),
        out_shape=one * panels,
        compiler_params=params(44),
        cost_estimate=cost(8 * panels * rows * order * width, 2 * order * order),
        name="product",
    )(at, a4, own, other)
    return [outs[4 * p : 4 * p + 4] for p in range(panels)]


def middle_kernel(panels, base, *refs):
    at_ref, refs = refs[0], refs[1:]
    keeps, refs = refs[:panels], refs[panels:]
    parts, refs = refs[: 3 * panels], refs[3 * panels :]
    masked, refs = refs[:4], refs[4:]
    own_ref, *coded = refs[:4]
    mine_ref, theirs_ref, sum_ref, m_ref = refs[4:]
    shard = own_ref.shape[0] // panels
    half = mine_ref.shape[0] // panels
    core, l = at_ref[1], at_ref[4]

    def place(k):
        return pl.ds(pl.multiple_of((l ^ k) * shard, 32), shard)

    for p in range(panels):
        value = keeps[p][...]
        for ref in parts[3 * p : 3 * p + 3]:
            value = value + decode(ref)
        sum_ref[...] = value
        own_ref[p * shard : (p + 1) * shard, :] = sum_ref[place(0), :]
        for k in (1, 2, 3):
            encode(sum_ref[place(k), :], coded[k - 1], p * (shard + EXTRA))
        for k, ref in enumerate(masked):
            m_ref[place(k), :] = ref[base + p]
        high = value.astype(BF16)
        rest = value - high.astype(F32)
        mid = rest.astype(BF16)
        low = (rest - mid.astype(F32)).astype(BF16)
        for which, out in ((core, mine_ref), (1 - core, theirs_ref)):
            left = m_ref[:, pl.ds(pl.multiple_of(which * half, 128), half)]
            dims = (((0,), (0,)), ((), ()))
            terms = [
                lax.dot_general(left, r, dims, preferred_element_type=F32) for r in (low, mid, high)
            ]
            out[p * half : (p + 1) * half, :] = (terms[0] + terms[1]) + terms[2]


def middle(at, keeps, parts, masked, base):
    rows, width = keeps[0].shape
    panels, shard = len(keeps), rows // 4
    return pl.pallas_call(
        functools.partial(middle_kernel, panels, base),
        in_specs=[SMEM] + [VMEM] * (4 * panels + 4),
        out_specs=[VMEM] * 6,
        out_shape=[jax.ShapeDtypeStruct((panels * shard, width), F32)]
        + [jax.ShapeDtypeStruct((panels * (shard + EXTRA), width), I16)] * 3
        + [jax.ShapeDtypeStruct((panels * (width // 2), width), F32)] * 2,
        scratch_shapes=[pltpu.VMEM((rows, width), F32), pltpu.VMEM((rows, width), BF16)],
        compiler_params=params(),
        cost_estimate=cost(6 * rows * width * width, 16 * rows * width),
        name="middle",
    )(at, *keeps, *sum(parts, []), *masked)


def last_kernel(groups, *refs):
    out_ref = refs[-1]
    shard = out_ref.shape[1]
    for g, which in enumerate(groups):
        own_ref, *parts = refs[4 * g : 4 * g + 4]
        for p, panel in enumerate(which):
            total = own_ref[p * shard : (p + 1) * shard, :]
            for ref in parts:
                total = total + decode(ref, p * (shard + EXTRA), shard)
            out_ref[panel] = -total


def last(groups, shape):
    ins = [ref for own, parts, _ in groups for ref in (own, *parts)]
    return pl.pallas_call(
        functools.partial(last_kernel, [which for _, _, which in groups]),
        in_specs=[VMEM] * len(ins),
        out_specs=VMEM,
        out_shape=jax.ShapeDtypeStruct(shape, F32),
        compiler_params=params(),
        cost_estimate=cost(8 * shape[1] * shape[2], 16 * shape[1] * shape[2]),
        name="last",
    )(*ins)


def encode_lanes(value, out_ref, start=0):
    rows, width = value.shape
    largest = jnp.maximum(jnp.max(jnp.abs(value), axis=1, keepdims=True), 1e-30)
    level = jnp.ceil(jnp.log(largest * (1.0 / TOP)) * (STEPS / LN2))
    coded = jnp.round(value * jnp.exp2(level * (-1.0 / STEPS)))
    out_ref[start : start + rows, :width] = coded.astype(I32).astype(I16)
    lanes = jnp.broadcast_to(level, (rows, LANES))
    out_ref[start : start + rows, width:] = lanes.astype(I32).astype(I16)


def decode_lanes(block):
    width = block.shape[1] - LANES
    coded = block[:, :width].astype(I32).astype(F32)
    level = block[:, width:].astype(I32).astype(F32)[:, :1]
    return coded * jnp.exp2(level * (1.0 / STEPS))


def fold_kernel(*refs):
    out, count = refs[-1], len(refs) // 2
    start = 0
    for p in range(count):
        rows = refs[p].shape[0]
        encode_lanes(refs[p][...] + refs[count + p][...], out, start)
        start += rows


def fold(mines, theirs):
    width = mines[0].shape[1]
    total = sum(mine.shape[0] for mine in mines)
    return pl.pallas_call(
        fold_kernel,
        in_specs=[VMEM] * (2 * len(mines)),
        out_specs=VMEM,
        out_shape=jax.ShapeDtypeStruct((total, width + LANES), I16),
        compiler_params=params(),
        cost_estimate=cost(total * width, 12 * total * width),
        name="fold",
    )(*mines, *theirs)


def gathered_kernel(in_ref, out_ref):
    total = decode_lanes(in_ref[0])
    for k in range(1, in_ref.shape[0]):
        total = total + decode_lanes(in_ref[k])
    out_ref[...] = total


def gathered(pieces):
    count, rows, lanes = pieces.shape
    return pl.pallas_call(
        gathered_kernel,
        in_specs=[VMEM],
        out_specs=VMEM,
        out_shape=jax.ShapeDtypeStruct((rows, lanes - LANES), F32),
        compiler_params=params(),
        cost_estimate=cost(count * rows * lanes, 2 * count * rows * lanes),
        name="gathered",
    )(pieces)


def copies_kernel(own_ref, r1_ref, r2_ref, r3_ref, out_ref):
    total = (own_ref[...] + r1_ref[...]) + (r2_ref[...] + r3_ref[...])
    encode_lanes(total, out_ref.at[0])
    for k in range(1, out_ref.shape[0]):
        out_ref[k] = out_ref[0]


def copies(own, found):
    rows, width = own.shape
    return pl.pallas_call(
        copies_kernel,
        in_specs=[VMEM] * 4,
        out_specs=VMEM,
        out_shape=jax.ShapeDtypeStruct((16, rows, width + LANES), I16),
        compiler_params=params(),
        cost_estimate=cost(rows * width, 32 * rows * width),
        name="copies",
    )(own, *found)


def finish_kernel(at_ref, mine_ref, theirs_ref, diag_ref, out_ref):
    half = mine_ref.shape[0]
    core = at_ref[1]
    for which, ref in ((core, mine_ref), (1 - core, theirs_ref)):
        place = pl.ds(pl.multiple_of(which * half, 8), half)
        out_ref[0, place, :] = diag_ref[0, place, :] + decode_lanes(ref[...])


def finish(at, mine, theirs, diag):
    panels, rows, width = diag.shape
    coded = pl.BlockSpec((rows // 2, width + LANES), lambda p, s: (p, 0))
    whole = pl.BlockSpec((1, rows, width), lambda p, s: (p, 0, 0))
    return pl.pallas_call(
        finish_kernel,
        grid_spec=pltpu.PrefetchScalarGridSpec(
            num_scalar_prefetch=1,
            grid=(panels,),
            in_specs=[coded, coded, whole],
            out_specs=whole,
        ),
        out_shape=jax.ShapeDtypeStruct(diag.shape, F32),
        compiler_params=params(54),
        cost_estimate=cost(diag.size, 12 * diag.size),
        name="finish",
    )(at, mine, theirs, diag)


def after(values, *earlier):
    return lax.optimization_barrier((values, earlier))[0]


def body(ancestor_inverse, panels, diag_inverse, tile_mask):
    x, h, core, l, y = (lax.axis_index(axis) for axis in AXES)
    at = jnp.stack([y, core, h, x ^ l, l, x]).astype(I32)
    kept, count, width = panels.shape
    order = ancestor_inverse.shape[1]
    tiles = tile_mask.shape[1]
    start = (((x * 2 + h) * 2 + core) * 16 + l * 4 + y) * kept
    tile = start // TILE
    first = lax.dynamic_slice_in_dim(tile_mask, tile, 1, 1)
    second = lax.dynamic_slice_in_dim(tile_mask, jnp.minimum(tile + 1, tiles - 1), 1, 1)
    in_first = start + jnp.arange(kept) < (tile + 1) * TILE
    own_mask = jnp.where(in_first[None, :], first, second).astype(BF16)
    masked = jnp.swapaxes(panels, 0, 1) * own_mask[:, :, None]

    def gather(message):
        return [message] + [send(message, over_x(k)) for k in (1, 2, 3)]

    a4 = ancestor_inverse.reshape(4, 4, kept, order)
    moved_a, moved_b = send(masked[2:], spread), send(masked[:2], spread)
    turned_a = [send(moved_a, turn(i)) for i in range(2)]
    turned_b = [send(moved_b, turn(i)) for i in range(2)]
    own_a = gather(after(jnp.stack(turned_a), moved_b))
    own_a = after(jnp.stack(own_a), turned_b)
    own_b = gather(after(jnp.stack(turned_b), own_a))
    ((keep_a, *coded),) = product(at, a4, own_a, send(own_a, over_core))
    parts_a = [send(coded[k - 1], over_y(k)) for k in (1, 2, 3)]
    far = send(after(masked, own_a), over_l(2))
    own_b = after(jnp.stack(own_b), parts_a[0], parts_a[2], far)
    other_b = send(own_b, over_core)
    ((keep_b, *coded),) = product(at, a4, own_b, other_b)
    parts_b = [send(q, over_y(k)) for k, q in zip((1, 2, 3), after(coded, parts_a[0], parts_a[2]))]
    ((keep_c, *coded),) = product(at, a4, own_b, other_b, 1)
    parts_c = [send(q, over_y(k)) for k, q in zip((1, 2, 3), coded)]
    late = after(masked, keep_c)
    beside = [masked, send(late, over_l(1)), far, send(late, over_l(3))]
    parts_b = after(parts_b, keep_c)
    own_2, *coded = middle(at, [keep_a], [after(parts_a, parts_b)], beside, 2)
    coded_2, (mine_2, their_2) = coded[:3], coded[3:]
    swapped_2 = send(their_2, over_core)
    found_2 = [send(coded_2[k - 1], over_l(k)) for k in (1, 2, 3)]
    parts_c = after(parts_c, mine_2)
    own_01, *coded = middle(at, [keep_b, keep_c], [parts_b, parts_c], beside, 0)
    coded_01, (mine_01, their_01) = coded[:3], coded[3:]
    swapped_01 = send(their_01, over_core)
    halves = fold([mine_01, mine_2], [swapped_01, swapped_2])
    found_01 = [send(coded_01[k - 1], over_l(k)) for k in (1, 2, 3)]
    pieces = halves.reshape(16, -1, width + LANES)
    total = gathered(lax.all_to_all(pieces, ("x", "y"), 0, 0))
    found_01 = after(found_01, total)
    total = total + send(total, over_h)
    beyond = [send(total, over_l(k)) for k in (1, 2, 3)]
    pieces = copies(total, after(beyond, found_01))
    mine = after(lax.all_to_all(pieces, ("x", "y"), 0, 0), found_2).reshape(halves.shape)
    blocks = last([(own_01, found_01, (0, 1)), (own_2, found_2, (2,))], masked.shape)
    diagonal = finish(at, mine, send(mine, over_core), diag_inverse)
    return jnp.swapaxes(blocks, 0, 1), diagonal


def solution(mesh):
    finer = Mesh(mesh.devices.reshape(SIZES), AXES)
    placed = (P(ROW, COL), P(AXES, None, None), P(), P())
    return jax.shard_map(
        body, mesh=finer, in_specs=placed, out_specs=(P(AXES, None, None), P()), check_vma=False
    )
```

```python
import functools

import jax
import jax.numpy as jnp
from jax import lax
from jax.experimental import pallas as pl
from jax.experimental.pallas import tpu as pltpu
from jax.sharding import Mesh
from jax.sharding import PartitionSpec as P

TILE = 128
AXES = ("x", "h", "core", "l", "y")
SIZES = (4, 2, 2, 4, 4)
ROW = ("x", "h", "core")
COL = ("l", "y")
EXTRA = 16
LANES = 128
STEPS = 64.0
TOP = 32766.0
LN2 = 0.6931471805599453
VMEM = pl.BlockSpec(memory_space=pltpu.VMEM)
SMEM = pl.BlockSpec(memory_space=pltpu.SMEM)
F32, BF16, I16, I32 = jnp.float32, jnp.bfloat16, jnp.int16, jnp.int32


def coords(device):
    out = []
    for size in SIZES[::-1]:
        out.append(device % size)
        device //= size
    return tuple(out[::-1])


def number(place):
    value = 0
    for size, at in zip(SIZES, place):
        value = value * size + at
    return value


def send(value, move):
    pairs = [(d, number(move(*coords(d)))) for d in range(256)]
    return lax.ppermute(value, AXES, pairs)


def over_x(k):
    return lambda x, h, c, l, y: (x ^ k, h, c, l, y)


def over_y(k):
    return lambda x, h, c, l, y: (x, h, c, l, y ^ k)


def over_l(k):
    return lambda x, h, c, l, y: (x, h, c, l ^ k, y)


def over_h(x, h, c, l, y):
    return (x, 1 - h, c, l, y)


def over_core(x, h, c, l, y):
    return (x, h, 1 - c, l, y)


def spread(x, h, c, l, y):
    return (x ^ l, h, c, l, y)


def turn(i):
    return lambda x, h, c, l, y: (x, (y & 1) ^ i, y >> 1, x ^ l, 2 * h + c)


def params(limit=20):
    return pltpu.CompilerParams(vmem_limit_bytes=limit * 1024 * 1024)


def cost(flops, moved):
    return pl.CostEstimate(flops=flops // 1000, bytes_accessed=moved // 1000, transcendentals=0)


def diagonal_mask(rows, width):
    row = lax.broadcasted_iota(I32, (rows, width), 0)
    lane = lax.broadcasted_iota(I32, (rows, width), 1)
    return row == lane


def encode(value, out_ref, start=0):
    rows, width = value.shape
    largest = jnp.maximum(jnp.max(jnp.abs(value), axis=1, keepdims=True), 1e-30)
    level = jnp.ceil(jnp.log(largest * (1.0 / TOP)) * (STEPS / LN2))
    coded = jnp.round(value * jnp.exp2(level * (-1.0 / STEPS)))
    out_ref[start : start + rows, :] = coded.astype(I32).astype(I16)
    line = jnp.sum(jnp.where(diagonal_mask(rows, width), level, 0.0), axis=0, keepdims=True)
    lines = jnp.broadcast_to(line, (EXTRA, width))
    out_ref[start + rows : start + rows + EXTRA, :] = lines.astype(I32).astype(I16)


def decode(in_ref, start=0, rows=None):
    rows, width = rows or in_ref.shape[0] - EXTRA, in_ref.shape[1]
    coded = in_ref[start : start + rows, :].astype(I32).astype(F32)
    line = in_ref[start + rows : start + rows + EXTRA, :].astype(I32).astype(F32)[:1]
    level = jnp.sum(
        jnp.where(diagonal_mask(rows, width), jnp.broadcast_to(line, (rows, width)), 0.0),
        axis=1,
        keepdims=True,
    )
    return coded * jnp.exp2(level * (1.0 / STEPS))


def product_kernel(panels, at_ref, a_ref, own_ref, other_ref, *refs):
    outs, m_ref = refs[: 4 * panels], refs[4 * panels]
    step = pl.program_id(0)
    shard = own_ref.shape[3]

    @pl.when(step == 0)
    def _():
        core, h, t = at_ref[1], at_ref[2], at_ref[3]
        for p in range(panels):
            for k in range(4):
                for i in range(2):
                    base = (k ^ t) * (4 * shard) + (i ^ h) * shard
                    first = pl.multiple_of(base + core * (2 * shard), 32)
                    second = pl.multiple_of(base + (1 - core) * (2 * shard), 32)
                    m_ref[p, pl.ds(first, shard), :] = own_ref[k, i, p]
                    m_ref[p, pl.ds(second, shard), :] = other_ref[k, i, p]

    block = a_ref[...]
    lines = block.reshape(4 * block.shape[2], block.shape[3])
    for p in range(panels):
        value = jnp.dot(lines, m_ref[p], preferred_element_type=F32)
        for at in range(3):

            @pl.when(step == at)
            def _(ref=outs[4 * p + 1 + at], value=value):
                encode(value, ref)

        @pl.when(step == 3)
        def _(ref=outs[4 * p], value=value):
            ref[...] = value


def product(at, a4, own, other, first=0):
    shard, order = a4.shape[2], a4.shape[3]
    panels, width = 1, own.shape[4]
    rows = 4 * shard
    whole = pl.BlockSpec((4, 2, panels, shard, width), lambda g, s: (0, 0, first, 0, 0))
    kept = pl.BlockSpec((rows, width), lambda g, s: (0, 0))
    coded = pl.BlockSpec((rows + EXTRA, width), lambda g, s: (0, 0))
    one = [jax.ShapeDtypeStruct((rows, width), F32)]
    one += [jax.ShapeDtypeStruct((rows + EXTRA, width), I16)] * 3
    outs = pl.pallas_call(
        functools.partial(product_kernel, panels),
        grid_spec=pltpu.PrefetchScalarGridSpec(
            num_scalar_prefetch=1,
            grid=(4,),
            in_specs=[
                pl.BlockSpec(
                    (4, 1, shard, order), lambda g, s: (0, s[0] ^ ((g + 1) & 3), 0, 0)
                ),
                whole,
                whole,
            ],
            out_specs=([kept] + [coded] * 3) * panels,
            scratch_shapes=[pltpu.VMEM((panels, order, width), BF16)],
        ),
        out_shape=one * panels,
        compiler_params=params(44),
        cost_estimate=cost(8 * panels * rows * order * width, 2 * order * order),
        name="product",
    )(at, a4, own, other)
    return [outs[4 * p : 4 * p + 4] for p in range(panels)]


def middle_kernel(panels, base, *refs):
    at_ref, refs = refs[0], refs[1:]
    keeps, refs = refs[:panels], refs[panels:]
    parts, refs = refs[: 3 * panels], refs[3 * panels :]
    masked, refs = refs[:4], refs[4:]
    own_ref, *coded = refs[:4]
    mine_ref, theirs_ref, sum_ref, m_ref = refs[4:]
    shard = own_ref.shape[0] // panels
    half = mine_ref.shape[0] // panels
    core, l = at_ref[1], at_ref[4]

    def place(k):
        return pl.ds(pl.multiple_of((l ^ k) * shard, 32), shard)

    for p in range(panels):
        value = keeps[p][...]
        for ref in parts[3 * p : 3 * p + 3]:
            value = value + decode(ref)
        sum_ref[...] = value
        own_ref[p * shard : (p + 1) * shard, :] = sum_ref[place(0), :]
        for k in (1, 2, 3):
            encode(sum_ref[place(k), :], coded[k - 1], p * (shard + EXTRA))
        for k, ref in enumerate(masked):
            m_ref[place(k), :] = ref[base + p]
        high = value.astype(BF16)
        rest = value - high.astype(F32)
        mid = rest.astype(BF16)
        low = (rest - mid.astype(F32)).astype(BF16)
        for which, out in ((core, mine_ref), (1 - core, theirs_ref)):
            left = m_ref[:, pl.ds(pl.multiple_of(which * half, 128), half)]
            dims = (((0,), (0,)), ((), ()))
            terms = [
                lax.dot_general(left, r, dims, preferred_element_type=F32) for r in (low, mid, high)
            ]
            out[p * half : (p + 1) * half, :] = (terms[0] + terms[1]) + terms[2]


def middle(at, keeps, parts, masked, base):
    rows, width = keeps[0].shape
    panels, shard = len(keeps), rows // 4
    return pl.pallas_call(
        functools.partial(middle_kernel, panels, base),
        in_specs=[SMEM] + [VMEM] * (4 * panels + 4),
        out_specs=[VMEM] * 6,
        out_shape=[jax.ShapeDtypeStruct((panels * shard, width), F32)]
        + [jax.ShapeDtypeStruct((panels * (shard + EXTRA), width), I16)] * 3
        + [jax.ShapeDtypeStruct((panels * (width // 2), width), F32)] * 2,
        scratch_shapes=[pltpu.VMEM((rows, width), F32), pltpu.VMEM((rows, width), BF16)],
        compiler_params=params(),
        cost_estimate=cost(6 * rows * width * width, 16 * rows * width),
        name="middle",
    )(at, *keeps, *sum(parts, []), *masked)


def last_kernel(groups, *refs):
    out_ref = refs[-1]
    shard = out_ref.shape[1]
    for g, which in enumerate(groups):
        own_ref, *parts = refs[4 * g : 4 * g + 4]
        for p, panel in enumerate(which):
            total = own_ref[p * shard : (p + 1) * shard, :]
            for ref in parts:
                total = total + decode(ref, p * (shard + EXTRA), shard)
            out_ref[panel] = -total


def last(groups, shape):
    ins = [ref for own, parts, _ in groups for ref in (own, *parts)]
    return pl.pallas_call(
        functools.partial(last_kernel, [which for _, _, which in groups]),
        in_specs=[VMEM] * len(ins),
        out_specs=VMEM,
        out_shape=jax.ShapeDtypeStruct(shape, F32),
        compiler_params=params(),
        cost_estimate=cost(8 * shape[1] * shape[2], 16 * shape[1] * shape[2]),
        name="last",
    )(*ins)


def encode_lanes(value, out_ref, start=0):
    rows, width = value.shape
    largest = jnp.maximum(jnp.max(jnp.abs(value), axis=1, keepdims=True), 1e-30)
    level = jnp.ceil(jnp.log(largest * (1.0 / TOP)) * (STEPS / LN2))
    coded = jnp.round(value * jnp.exp2(level * (-1.0 / STEPS)))
    out_ref[start : start + rows, :width] = coded.astype(I32).astype(I16)
    lanes = jnp.broadcast_to(level, (rows, LANES))
    out_ref[start : start + rows, width:] = lanes.astype(I32).astype(I16)


def decode_lanes(block):
    width = block.shape[1] - LANES
    coded = block[:, :width].astype(I32).astype(F32)
    level = block[:, width:].astype(I32).astype(F32)[:, :1]
    return coded * jnp.exp2(level * (1.0 / STEPS))


def fold_kernel(*refs):
    out, count = refs[-1], len(refs) // 2
    start = 0
    for p in range(count):
        rows = refs[p].shape[0]
        encode_lanes(refs[p][...] + refs[count + p][...], out, start)
        start += rows


def fold(mines, theirs):
    width = mines[0].shape[1]
    total = sum(mine.shape[0] for mine in mines)
    return pl.pallas_call(
        fold_kernel,
        in_specs=[VMEM] * (2 * len(mines)),
        out_specs=VMEM,
        out_shape=jax.ShapeDtypeStruct((total, width + LANES), I16),
        compiler_params=params(),
        cost_estimate=cost(total * width, 12 * total * width),
        name="fold",
    )(*mines, *theirs)


def gathered_kernel(in_ref, out_ref):
    total = decode_lanes(in_ref[0])
    for k in range(1, in_ref.shape[0]):
        total = total + decode_lanes(in_ref[k])
    out_ref[...] = total


def gathered(pieces):
    count, rows, lanes = pieces.shape
    return pl.pallas_call(
        gathered_kernel,
        in_specs=[VMEM],
        out_specs=VMEM,
        out_shape=jax.ShapeDtypeStruct((rows, lanes - LANES), F32),
        compiler_params=params(),
        cost_estimate=cost(count * rows * lanes, 2 * count * rows * lanes),
        name="gathered",
    )(pieces)


def copies_kernel(own_ref, other_ref, out_ref):
    encode_lanes(own_ref[...] + other_ref[...], out_ref.at[0])
    for k in range(1, out_ref.shape[0]):
        out_ref[k] = out_ref[0]


def copies(own, found):
    rows, width = own.shape
    return pl.pallas_call(
        copies_kernel,
        in_specs=[VMEM] * 2,
        out_specs=VMEM,
        out_shape=jax.ShapeDtypeStruct((16, rows, width + LANES), I16),
        compiler_params=params(),
        cost_estimate=cost(rows * width, 32 * rows * width),
        name="copies",
    )(own, found)


def finish_kernel(at_ref, mine_ref, theirs_ref, diag_ref, out_ref):
    half = diag_ref.shape[1] // 2
    core = at_ref[1]
    for p in range(diag_ref.shape[0]):
        for which, ref in ((core, mine_ref), (1 - core, theirs_ref)):
            place = pl.ds(pl.multiple_of(which * half, 8), half)
            part = decode_lanes(ref[p * half : (p + 1) * half, :])
            out_ref[p, place, :] = diag_ref[p, place, :] + part


def finish(at, mine, theirs, diag):
    return pl.pallas_call(
        finish_kernel,
        in_specs=[SMEM] + [VMEM] * 3,
        out_specs=VMEM,
        out_shape=jax.ShapeDtypeStruct(diag.shape, F32),
        compiler_params=params(),
        cost_estimate=cost(diag.size, 12 * diag.size),
        name="finish",
    )(at, mine, theirs, diag)


def after(values, *earlier):
    return lax.optimization_barrier((values, earlier))[0]


def body(ancestor_inverse, panels, diag_inverse, tile_mask):
    x, h, core, l, y = (lax.axis_index(axis) for axis in AXES)
    at = jnp.stack([y, core, h, x ^ l, l, x]).astype(I32)
    kept, count, width = panels.shape
    order = ancestor_inverse.shape[1]
    tiles = tile_mask.shape[1]
    start = (((x * 2 + h) * 2 + core) * 16 + l * 4 + y) * kept
    tile = start // TILE
    first = lax.dynamic_slice_in_dim(tile_mask, tile, 1, 1)
    second = lax.dynamic_slice_in_dim(tile_mask, jnp.minimum(tile + 1, tiles - 1), 1, 1)
    in_first = start + jnp.arange(kept) < (tile + 1) * TILE
    own_mask = jnp.where(in_first[None, :], first, second).astype(BF16)
    masked = jnp.swapaxes(panels, 0, 1) * own_mask[:, :, None]

    def gather(message):
        return [message] + [send(message, over_x(k)) for k in (1, 2, 3)]

    a4 = ancestor_inverse.reshape(4, 4, kept, order)
    moved_a, moved_b = send(masked[2:], spread), send(masked[:2], spread)
    turned_a = [send(moved_a, turn(i)) for i in range(2)]
    turned_b = [send(moved_b, turn(i)) for i in range(2)]
    own_a = gather(after(jnp.stack(turned_a), moved_b))
    own_a = after(jnp.stack(own_a), turned_b)
    own_b = gather(after(jnp.stack(turned_b), own_a))
    ((keep_a, *coded),) = product(at, a4, own_a, send(own_a, over_core))
    parts_a = [send(coded[k - 1], over_y(k)) for k in (1, 2, 3)]
    far = send(after(masked, own_a), over_l(2))
    own_b = after(jnp.stack(own_b), parts_a[0], parts_a[2])
    other_b = send(own_b, over_core)
    ((keep_b, *coded),) = product(at, a4, own_b, other_b)
    parts_b = [send(q, over_y(k)) for k, q in zip((1, 2, 3), after(coded, parts_a[0], parts_a[2]))]
    ((keep_c, *coded),) = product(after(at, far), a4, own_b, other_b, 1)
    parts_c = [send(q, over_y(k)) for k, q in zip((1, 2, 3), coded)]
    late = after(masked, keep_c)
    beside = [masked, send(late, over_l(1)), far, send(late, over_l(3))]
    parts_b = after(parts_b, keep_c)
    own_2, *coded = middle(at, [keep_a], [after(parts_a, parts_b)], beside, 2)
    coded_2, (mine_2, their_2) = coded[:3], coded[3:]
    swapped_2 = send(their_2, over_core)
    found_2 = [send(coded_2[k - 1], over_l(k)) for k in (1, 2, 3)]
    parts_c = after(parts_c, mine_2)
    own_01, *coded = middle(at, [keep_b, keep_c], [parts_b, parts_c], beside, 0)
    coded_01, (mine_01, their_01) = coded[:3], coded[3:]
    swapped_01 = send(their_01, over_core)
    halves = fold([mine_01, mine_2], [swapped_01, swapped_2])
    found_01 = [send(coded_01[k - 1], over_l(k)) for k in (1, 2, 3)]
    pieces = halves.reshape(16, -1, width + LANES)
    total = gathered(lax.all_to_all(pieces, ("x", "y"), 0, 0))
    found_01 = after(found_01, total)
    near = [send(total, over_l(k)) for k in (1, 2, 3)]
    total = (total + near[0]) + (near[1] + near[2])
    pieces = copies(total, after(send(total, over_h), found_01))
    mine = after(lax.all_to_all(pieces, ("x", "y"), 0, 0), found_2).reshape(halves.shape)
    blocks = last([(own_01, found_01, (0, 1)), (own_2, found_2, (2,))], masked.shape)
    diagonal = finish(at, mine, send(mine, over_core), diag_inverse)
    return jnp.swapaxes(blocks, 0, 1), diagonal


def solution(mesh):
    finer = Mesh(mesh.devices.reshape(SIZES), AXES)
    placed = (P(ROW, COL), P(AXES, None, None), P(), P())
    return jax.shard_map(
        body, mesh=finer, in_specs=placed, out_specs=(P(AXES, None, None), P()), check_vma=False
    )
```
